512 devices in a mesh: row: 32 (over x, y, core), col: 16 (over z).
Axes of the slice: x: 4, y: 4, z: 16, core: 2. Of those that a mesh axis runs over, the one named last changes fastest.
Arguments:
- tokens: bfloat16 [4096, 2560], P('row', 'col'), may hold values from -6 to 6
- w_gate: bfloat16 [512, 192, 2560], P(('row', 'col')), may hold values from -0.125 to 0.125
- w_up: bfloat16 [512, 192, 2560], P(('row', 'col')), may hold values from -0.125 to 0.125
- w_down: bfloat16 [512, 192, 2560], P(('row', 'col')), may hold values from -0.15625 to 0.15625
- adp_down: bfloat16 [64, 16, 2560], P('row', None, 'col'), may hold values from -0.125 to 0.125
- adp_up: bfloat16 [64, 16, 2560], P('row', None, 'col'), may hold values from -1.5 to 1.5
- expert_ids: int32 [4096, 6], P('row'), may hold values from 0 to 63, all different within a row; in each aligned block of 128 rows (0 to 127, 128 to 255, ...) at most 16 rows name the same one
- gate_vals: float32 [4096, 6], P('row'), may hold values from 0.05 to 0.5
- lengths: int32 [16], replicated, may hold values from 1 to 1365, 4096 in all
- perm: int32 [4096], P('row'), may hold values from 0 to 4095, each once
- req_adapter: int32 [16], replicated, may hold values from 0 to 63
Outputs:
- layer_out: bfloat16 [4096, 2560], P('row', 'col')
The draws below stay inside these ranges and needn't reach their ends.
Inputs may be any that keep to these rules, and one draw needn't show every extreme that they name: `expert_ids`: within the 128 rows of one index of row, no expert is named by more than 16 rows, a bound that some block reaches; each row names 6 different experts. `perm`: each position appears once. `lengths`: they sum to 4096; the longest is exactly 4096 // 3.
All inputs are finite; a program needn't handle non-finite values.
Results may differ from the reference program's by a relative error of at most 0.0051.
Values may be sent and summed in bfloat16 or wider, within the bound.
A program may use at most 128 MiB of HBM per device.

```python
import math
import jax
import jax.numpy as jnp
import numpy as np
from jax import lax

D = 2560
FF = 1536
TOPK = 6
EXPERTS = 64
SLICES = 8
RANK = 16
ADAPTERS = 64
REQS = 16
TOK_DEV = 128
TOKENS = 4096
CAP = 16
N_ROW = 32


def plant(array, key, smallest, largest):
    longest = array.shape.index(max(array.shape))
    spots = []
    for shift in (0, 1):
        where = [jax.random.randint(jax.random.fold_in(key, axis), (), 0, length) for axis, length in enumerate(array.shape)]
        where[longest] = (where[longest] + shift) % array.shape[longest]
        spots.append(tuple(where))
    return array.at[spots[0]].set(smallest).at[spots[1]].set(largest)


def shard_levels(rng, extent, cuts, smallest, high):
    loudness = 1.0
    for axis_at, blocks in cuts:
        heights = jax.random.uniform(jax.random.fold_in(jax.random.fold_in(rng, 6), axis_at), (blocks,), jnp.float32, smallest / len(cuts), high / len(cuts))
        loudness = loudness * jnp.repeat(jnp.exp(heights), extent[axis_at] // blocks).reshape((-1,) + (1,) * (len(extent) - 1 - axis_at))
    return loudness


def profile(amount, total, reach, slope):
    portions = [(1 << 20) // math.isqrt(rank ** slope) + 1 for rank in range(2, amount + 1)]
    rest, holding = total - reach - (amount - 1), [1] * (amount - 1)
    while rest > 0:
        candidates = [i for i in range(amount - 1) if holding[i] < reach]
        pool, left = sum([portions[i] for i in candidates]), rest
        for i in candidates:
            more = min(reach - holding[i], max(1, left * portions[i] // pool), rest)
            holding[i] = holding[i] + more
            rest = rest - more
    return np.array([reach] + holding)


def uneven(key, number_of, total, most, lean):
    if number_of == 2:
        one = jax.random.randint(key, (), max(1, total - most), min(most, total - 1) + 1)
        return jnp.stack([one, total - one])
    sizes = jnp.asarray(profile(number_of, total, most, lean), jnp.int32)
    pairs = (number_of - 1) // 2
    source_of, taker = sizes[1:1 + 2 * pairs:2], sizes[2:2 + 2 * pairs:2]
    margin = jnp.minimum(source_of - 1, most - taker)
    shifted = jax.random.randint(jax.random.fold_in(key, 1), (pairs,), 0, 1 << 20) % (margin + 1)
    sizes = sizes.at[1:1 + 2 * pairs:2].set(source_of - shifted).at[2:2 + 2 * pairs:2].set(taker + shifted)
    return sizes[jax.random.permutation(jax.random.fold_in(key, 2), number_of)]


def deal_out(key, own, number, rows, number_of, top, bound, skew):
    sequence = jax.random.permutation(key, number_of)
    packed, common = shares(number_of, rows * top, bound, skew, True), shares(number_of, rows * top, bound, skew, False)
    places = jnp.arange(number_of)

    def named(tallies, offset_by):
        used = int((tallies > 0).sum())
        fixed = max(1, used // 4)
        moved = fixed + (places - fixed + offset_by * (used - fixed)) % max(1, number_of - fixed)
        return jnp.zeros((number_of,), jnp.int32).at[sequence[jnp.where(places < fixed, places, moved)]].set(jnp.asarray(tallies, jnp.int32))

    tallies = jnp.where(number % 4 == 0, named(packed, number // 4), named(common, number - number // 4 - 1))
    mixed = jax.random.permutation(jax.random.fold_in(own, 3), number_of)
    donor, receiver = mixed[0:number_of // 2 * 2:2], mixed[1:number_of // 2 * 2:2]
    room = jnp.minimum(tallies[donor] - 1, bound - tallies[receiver]) // 2
    room = jnp.where((donor == sequence[0]) | (receiver == sequence[0]) | (tallies[receiver] == 0), 0, jnp.maximum(room, 0))
    moved = jax.random.randint(jax.random.fold_in(own, 4), (number_of // 2,), 0, 1 << 20) % (room + 1)
    tallies = tallies.at[donor].add(-moved).at[receiver].add(moved)
    labels = jnp.searchsorted(jnp.cumsum(tallies), jnp.arange(rows * top), side="right").astype(jnp.int32)
    table = labels.reshape(top, rows).T
    table = table[jax.random.permutation(jax.random.fold_in(own, 1), rows)]
    offset_by = jax.random.randint(jax.random.fold_in(own, 2), (rows, 1), 0, top)
    return jnp.take_along_axis(table, (jnp.arange(top)[None, :] + offset_by) % top, axis=1)


def shares(amount, total, limit, lean, full):
    loads = [(1 << 20) // math.isqrt(standing ** lean) + 1 for standing in range(1, amount + 1)]
    largest = limit if full else min(limit, max(-(-total // amount), total * loads[0] // sum(loads)))
    least = 1 if total - largest >= amount - 1 else 0
    holding, surplus = [largest] + [least] * (amount - 1), total - largest - least * (amount - 1)
    while surplus > 0:
        free = [i for i in range(1, amount) if holding[i] < largest] or [i for i in range(1, amount) if holding[i] < limit]
        mass, remaining = sum([loads[i] for i in free]), surplus
        for i in free:
            addition = min(limit - holding[i], max(1, remaining * loads[i] // mass), surplus)
            holding[i] = holding[i] + addition
            surplus = surplus - addition
    return np.array(holding)


def centred(own_key, extent, width, bound, cuts=(), held_as=jnp.bfloat16):
    values = width * jax.random.normal(own_key, extent, jnp.float32)
    if cuts:
        values = values * shard_levels(own_key, extent, cuts, -0.22, 0.18)
    return jnp.clip(values, -bound, bound).astype(held_as)


def setup_inputs(seed: int = 0) -> dict:
    key_of = jax.random.split(jax.random.key(seed), 12)
    tokens = centred(key_of[0], (TOKENS, D), 1.0, 6.0, ((0, 32), (1, 16)))
    w_gate = centred(key_of[1], (EXPERTS * SLICES, FF // SLICES, D), D ** -0.5, 0.125, ((0, 512),))
    w_up = centred(key_of[2], (EXPERTS * SLICES, FF // SLICES, D), D ** -0.5, 0.125, ((0, 512),))
    w_down = centred(key_of[3], (EXPERTS * SLICES, FF // SLICES, D), FF ** -0.5, 0.15625, ((0, 512),))
    adp_down = centred(key_of[4], (ADAPTERS, RANK, D), D ** -0.5, 0.125, ((0, 32), (2, 16)))
    adp_up = centred(key_of[5], (ADAPTERS, RANK, D), RANK ** -0.5, 1.5, ((0, 32), (2, 16)))
    expert_ids_keys = jax.random.split(jax.random.fold_in(key_of[6], 1), TOKENS // TOK_DEV)
    expert_ids_turns = jax.random.permutation(jax.random.fold_in(key_of[6], 3), TOKENS // TOK_DEV)
    expert_ids = jax.vmap(lambda own, number: deal_out(jax.random.fold_in(key_of[6], 2), own, number, TOK_DEV, EXPERTS, TOPK, CAP, 2))(expert_ids_keys, expert_ids_turns).reshape((TOKENS, TOPK))
    gate_vals = jnp.clip(jnp.exp(math.log(0.5) - 2.3025851 * jax.random.uniform(key_of[7], (TOKENS, TOPK), jnp.float32) ** shard_levels(key_of[7], (TOKENS, TOPK), ((0, 32),), -0.2, 0.2)), 0.05, 0.5)
    lengths = uneven(key_of[8], REQS, TOKENS, TOKENS // 3, 2).astype(jnp.int32)
    perm = jax.random.permutation(key_of[9], TOKENS).astype(jnp.int32)
    req_adapter = plant(jax.random.randint(key_of[10], (REQS,), 0, ADAPTERS), jax.random.fold_in(key_of[10], 1), 0, ADAPTERS - 1).astype(jnp.int32)
    return {"tokens": tokens, "w_gate": w_gate, "w_up": w_up, "w_down": w_down, "adp_down": adp_down, "adp_up": adp_up, "expert_ids": expert_ids, "gate_vals": gate_vals, "lengths": lengths, "perm": perm, "req_adapter": req_adapter}


adapter_scale_factor = 2.0


def reference(tokens, w_gate, w_up, w_down, adp_down, adp_up, expert_ids, gate_vals, lengths, perm, req_adapter):
    ids = expert_ids.reshape(N_ROW, TOK_DEV * TOPK)
    onehot = (ids[:, :, None] == jnp.arange(EXPERTS, dtype=jnp.int32)[None, None, :]).astype(jnp.int32)
    slot = jnp.sum(onehot * jnp.cumsum(onehot, axis=1), axis=2) - 1
    index = (jnp.arange(N_ROW, dtype=jnp.int32)[:, None] * CAP + slot).reshape(-1).astype(jnp.int32)
    flat_ids = expert_ids.reshape(-1)
    flat_g = gate_vals.reshape(-1)
    tok_of = (jnp.arange(TOKENS * TOPK, dtype=jnp.int32) // TOPK).astype(jnp.int32)
    selected_experts = tokens[tok_of]
    dump = N_ROW * CAP
    hid_slice = FF // SLICES
    gate_full_matrix = w_gate.reshape(EXPERTS, FF, D)
    up_all = w_up.reshape(EXPERTS, FF, D)
    down_all = w_down.reshape(EXPERTS, SLICES, hid_slice, D)

    def step(carry, stuff):
        expert, wg, wu, wd = stuff
        chosen = flat_ids == expert
        where_to = jnp.where(chosen, index, dump).astype(jnp.int32)
        buffer = jnp.zeros((dump + 1, D), jnp.bfloat16).at[where_to].set(selected_experts)
        gate = jnp.dot(buffer, wg.T, preferred_element_type=jnp.float32)
        upper = jnp.dot(buffer, wu.T, preferred_element_type=jnp.float32)
        hidden = (jax.nn.silu(gate) * upper).astype(jnp.bfloat16)
        pieces = jnp.einsum('nsh,shd->snd', hidden.reshape(dump + 1, SLICES, hid_slice).astype(jnp.float32),
                            wd.astype(jnp.float32), precision=lax.Precision.HIGHEST)
        pieces = lax.optimization_barrier(pieces.astype(jnp.bfloat16))
        result = jnp.sum(pieces.astype(jnp.float32), axis=0)
        weight = jnp.where(chosen, flat_g, jnp.float32(0.0))
        contrib = weight[:, None] * result[where_to]
        return carry + jnp.sum(contrib.reshape(TOKENS, TOPK, D), axis=1), None

    dispatched_tokens, _ = lax.scan(step, jnp.zeros((TOKENS, D), jnp.float32),
                         (jnp.arange(EXPERTS, dtype=jnp.int32), gate_full_matrix, up_all, down_all))
    ends = jnp.cumsum(lengths)
    request = jnp.sum((perm[:, None] >= ends[None, :]).astype(jnp.int32), axis=1)
    adapter = jnp.sum(jnp.where(request[:, None] == jnp.arange(REQS, dtype=jnp.int32)[None, :], req_adapter[None, :], 0), axis=1)
    onehot_a = (adapter[:, None] == jnp.arange(ADAPTERS, dtype=jnp.int32)[None, :]).astype(jnp.float32)
    projected = jnp.einsum('td,kd->tk', tokens, adp_down.reshape(ADAPTERS * RANK, D), preferred_element_type=jnp.float32)
    low = jnp.sum(projected.reshape(TOKENS, ADAPTERS, RANK) * onehot_a[:, :, None], axis=1).astype(jnp.bfloat16)
    expanded = (onehot_a.astype(jnp.bfloat16)[:, :, None] * low[:, None, :]).reshape(TOKENS, ADAPTERS * RANK)
    adapter_update = jnp.dot(expanded, adp_up.reshape(ADAPTERS * RANK, D), preferred_element_type=jnp.float32)
    return (dispatched_tokens + adapter_scale_factor * adapter_update).astype(jnp.bfloat16)
```

```python
import jax
import jax.numpy as jnp
from jax import lax
from jax.sharding import PartitionSpec as P

adapter_scale_factor = 2.0


def contract(left, right, left_dim, right_dim):
    return lax.dot_general(
        left, right, (((left_dim,), (right_dim,)), ((), ())), preferred_element_type=jnp.float32
    )


def split_pair(value):
    high = lax.reduce_precision(value, 8, 7)
    return high.astype(jnp.bfloat16), (value - high).astype(jnp.bfloat16)


def spread(value, axis_name):
    count = lax.axis_size(axis_name)
    copies = jnp.broadcast_to(value[None], (count,) + value.shape)
    return lax.all_to_all(copies, axis_name, split_axis=0, concat_axis=0, tiled=True)


def body(
    tokens,
    w_gate,
    w_up,
    w_down,
    adp_down,
    adp_up,
    expert_ids,
    gate_vals,
    lengths,
    perm,
    req_adapter,
):
    count_tok = tokens.shape[0]
    share = tokens.shape[1]
    rows_count = lax.axis_size("row")
    cols_count = lax.axis_size("col")
    experts = 2 * rows_count
    parts = cols_count // 2
    which = lax.axis_index("col") // parts
    topk = expert_ids.shape[1]
    capacity = max(2, (4 * count_tok * topk + 3 * experts - 1) // (3 * experts))
    slots = rows_count * capacity
    features = cols_count * share
    rank = adp_down.shape[1]
    own_adapters = adp_down.shape[0]
    adapters = own_adapters * rows_count

    tokens_t = tokens.T
    full_t = spread(tokens_t, "col").reshape(features, count_tok)

    flat_ids = expert_ids.reshape(-1)
    onehot = (flat_ids[:, None] == jnp.arange(experts, dtype=jnp.int32)[None, :]).astype(jnp.int32)
    slot = jnp.sum(onehot * jnp.cumsum(onehot, axis=0), axis=1) - 1
    place = jnp.where(flat_ids % 2 == which, (flat_ids // 2) * capacity + slot, slots)
    place = place.reshape(count_tok, topk).T
    targets = jnp.arange(slots, dtype=jnp.int32)
    hit = targets[:, None, None] == place[None, :, :]
    dispatch = jnp.any(hit, axis=1).astype(jnp.bfloat16)
    combine = jnp.sum(jnp.where(hit, gate_vals.T[None, :, :], jnp.float32(0.0)), axis=1)
    combine = jnp.concatenate(split_pair(combine), axis=1)

    outgoing = contract(dispatch, full_t, 1, 1).astype(jnp.bfloat16)
    outgoing = outgoing.reshape(rows_count, capacity, features)
    mine = lax.all_to_all(outgoing, "row", split_axis=0, concat_axis=0, tiled=True)
    mine = mine.reshape(slots, features)
    gate = contract(mine, w_gate[0], 1, 1)
    upper = contract(mine, w_up[0], 1, 1)
    hidden = (jax.nn.silu(gate) * upper).astype(jnp.bfloat16)
    partial_out = contract(hidden, w_down[0], 1, 0).astype(jnp.bfloat16)
    partial_out = partial_out.reshape(rows_count, capacity, features)
    returned = lax.all_to_all(partial_out, "row", split_axis=0, concat_axis=0, tiled=True)
    returned = returned.reshape(slots, features)
    routed_t = contract(returned, combine, 0, 0)
    routed_t = (routed_t[:, :count_tok] + routed_t[:, count_tok:]).astype(jnp.bfloat16)

    maps = jnp.concatenate(
        [adp_down.reshape(own_adapters * rank, share), adp_up.reshape(own_adapters * rank, share)]
    )
    maps = spread(maps, "row").reshape(rows_count, 2, own_adapters * rank, share)
    down_all = maps[:, 0].reshape(adapters * rank, share)
    up_all = maps[:, 1].reshape(adapters * rank, share)
    nreq = lengths.shape[0]
    ends = jnp.cumsum(lengths)
    request = jnp.sum((perm[:, None] >= ends[None, :]).astype(jnp.int32), axis=1)
    adapter = jnp.sum(
        jnp.where(
            request[:, None] == jnp.arange(nreq, dtype=jnp.int32)[None, :], req_adapter[None, :], 0
        ),
        axis=1,
    )
    chosen = jnp.arange(adapters, dtype=jnp.int32)[:, None, None] == adapter[None, None, :]
    projected = contract(down_all, tokens_t, 1, 0).reshape(adapters, rank, count_tok)
    partial_low = jnp.sum(jnp.where(chosen, projected, jnp.float32(0.0)), axis=0)
    low_high, low_rest = split_pair(partial_low)

    extra = jnp.concatenate([low_high, low_rest])
    extra = jnp.broadcast_to(extra[None], (cols_count,) + extra.shape)
    sent = jnp.concatenate([routed_t.reshape(cols_count, share, count_tok), extra], axis=1)
    arrived = lax.all_to_all(sent, "col", split_axis=0, concat_axis=0, tiled=True)
    total = jnp.sum(arrived.astype(jnp.float32), axis=0)
    low = (total[share : share + rank] + total[share + rank :]).astype(jnp.bfloat16)
    expanded = jnp.where(chosen, low[None], jnp.bfloat16(0.0)).reshape(adapters * rank, count_tok)
    delta_t = contract(up_all, expanded, 0, 0)
    return (total[:share] + adapter_scale_factor * delta_t).T.astype(jnp.bfloat16)


def solution(mesh):
    in_specs = (
        P("row", "col"),
        P(("row", "col"), None, None),
        P(("row", "col"), None, None),
        P(("row", "col"), None, None),
        P("row", None, "col"),
        P("row", None, "col"),
        P("row", None),
        P("row", None),
        P(),
        P("row"),
        P(),
    )
    out_specs = P("row", "col")
    return jax.shard_map(body, mesh=mesh, in_specs=in_specs, out_specs=out_specs, check_vma=False)
```

```python
import functools

import jax
import jax.numpy as jnp
from jax import lax
from jax.experimental import pallas as pl
from jax.experimental.pallas import tpu as pltpu
from jax.sharding import PartitionSpec as P

MESH = pl.DeviceIdType.MESH
VMEM = pl.BlockSpec(memory_space=pltpu.VMEM)

adapter_scale_factor = 2.0


def contract(left, right, left_dim, right_dim):
    return lax.dot_general(
        left, right, (((left_dim,), (right_dim,)), ((), ())), preferred_element_type=jnp.float32
    )


def split_pair(value):
    high = lax.reduce_precision(value, 8, 7)
    return high.astype(jnp.bfloat16), (value - high).astype(jnp.bfloat16)


def remote(src, dst, send_sem, recv_sem, axis_name, peer):
    return pltpu.make_async_remote_copy(
        src_ref=src,
        dst_ref=dst,
        send_sem=send_sem,
        recv_sem=recv_sem,
        device_id={axis_name: peer},
        device_id_type=MESH,
    )


def gather_kernel(
    rows, cols, tok_ref, maps_ref, full_ref, all_ref, own_sem, ring_send, ring_recv, row_send, row_recv
):
    me_r, me_c = lax.axis_index("row"), lax.axis_index("col")
    sides = (lax.rem(me_c + 1, cols), lax.rem(me_c + cols - 1, cols))
    hops = (cols // 2, cols - 1 - cols // 2)

    barrier = pltpu.get_barrier_semaphore()
    for side in sides:
        pl.semaphore_signal(barrier, inc=1, device_id={"col": side}, device_id_type=MESH)

    def greet(away, carry):
        peer = lax.rem(me_r + away, rows)
        pl.semaphore_signal(barrier, inc=1, device_id={"row": peer}, device_id_type=MESH)
        return carry

    lax.fori_loop(1, rows, greet, 0)
    pl.semaphore_wait(barrier, rows + 1)

    def shard(way, step):
        return lax.rem(me_c + cols - step, cols) if way == 0 else lax.rem(me_c + step, cols)

    def sending(way, step):
        at = full_ref.at[shard(way, step)]
        src = tok_ref if step == 0 else at
        return remote(src, at, ring_send.at[way, step], ring_recv.at[way, step], "col", sides[way])

    def arriving(way, step):
        at = full_ref.at[shard(way, step + 1)]
        return remote(at, at, ring_send.at[way, step], ring_recv.at[way, step], "col", sides[way])

    def row_copy(away, owner):
        at = all_ref.at[owner]
        peer = lax.rem(me_r + away, rows)
        return remote(maps_ref, at, row_send.at[away], row_recv.at[away], "row", peer)

    for way in range(2):
        sending(way, 0).start()

    def row_start(away, carry):
        row_copy(away, me_r).start()
        return carry

    lax.fori_loop(1, rows, row_start, 0)
    own = (
        pltpu.make_async_copy(tok_ref, full_ref.at[me_c], own_sem.at[0]),
        pltpu.make_async_copy(maps_ref, all_ref.at[me_r], own_sem.at[1]),
    )
    for copy in own:
        copy.start()
    for step in range(max(hops)):
        for way in range(2):
            if step < hops[way]:
                arriving(way, step).wait_recv()
                if step + 1 < hops[way]:
                    sending(way, step + 1).start()
    for copy in own:
        copy.wait()
    for way in range(2):
        for step in range(hops[way]):
            sending(way, step).wait_send()

    def row_end(away, carry):
        copy = row_copy(away, lax.rem(me_r + rows - away, rows))
        copy.wait_recv()
        copy.wait_send()
        return carry

    lax.fori_loop(1, rows, row_end, 0)


def gather(tokens_t, maps):
    rows, cols = lax.axis_size("row"), lax.axis_size("col")
    return pl.pallas_call(
        functools.partial(gather_kernel, rows, cols),
        out_shape=(
            jax.ShapeDtypeStruct((cols,) + tokens_t.shape, tokens_t.dtype),
            jax.ShapeDtypeStruct((rows,) + maps.shape, maps.dtype),
        ),
        in_specs=[VMEM] * 2,
        out_specs=(VMEM, VMEM),
        scratch_shapes=[
            pltpu.SemaphoreType.DMA((2,)),
            pltpu.SemaphoreType.DMA((2, cols)),
            pltpu.SemaphoreType.DMA((2, cols)),
            pltpu.SemaphoreType.DMA((rows,)),
            pltpu.SemaphoreType.DMA((rows,)),
        ],
        compiler_params=pltpu.CompilerParams(collective_id=0, has_side_effects=True),
    )(tokens_t, maps)


def sum_kernel(
    cols, part_ref, low_ref, total_ref, low_total_ref,
    out_part, in_part, out_low, in_low, send_sem, recv_sem, low_send_sem, low_recv_sem,
):
    me = lax.axis_index("col")
    sides = (lax.rem(me + 1, cols), lax.rem(me + cols - 1, cols))
    half = cols // 2
    hops = (half, cols - 1 - half)

    barrier = pltpu.get_barrier_semaphore()
    for side in sides:
        pl.semaphore_signal(barrier, inc=1, device_id={"col": side}, device_id_type=MESH)
    pl.semaphore_wait(barrier, 2)

    def copies(way, step):
        return (
            remote(
                out_part.at[way, step], in_part.at[way, step],
                send_sem.at[way, step], recv_sem.at[way, step], "col", sides[way],
            ),
            remote(
                out_low.at[way, step], in_low.at[way, step],
                low_send_sem.at[way, step], low_recv_sem.at[way, step], "col", sides[way],
            ),
        )

    for step in range(max(hops)):
        for way in range(2):
            if step >= hops[way]:
                continue
            if way == 0:
                chunk = lax.rem(me + hops[0] - step, cols)
            else:
                chunk = lax.rem(me + cols - hops[1] + step, cols)
            value, low = part_ref[chunk], low_ref[...]
            if step > 0:
                for copy in copies(way, step - 1):
                    copy.wait_recv()
                value = value + in_part[way, step - 1].astype(jnp.float32)
                low = low + in_low[way, step - 1]
            out_part[way, step] = value.astype(jnp.bfloat16)
            out_low[way, step] = low
            for copy in copies(way, step):
                copy.start()
    total, low = part_ref[me], low_ref[...]
    for way in range(2):
        last = hops[way] - 1
        for copy in copies(way, last):
            copy.wait_recv()
        total = total + in_part[way, last].astype(jnp.float32)
        low = low + in_low[way, last]
    total_ref[...] = total
    low_total_ref[...] = low
    for way in range(2):
        for step in range(hops[way]):
            for copy in copies(way, step):
                copy.wait_send()


def sum_shares(parts, low):
    cols, share, count_tok = parts.shape
    hops = cols // 2
    slots = (2, hops, share, count_tok)
    low_slots = (2, hops) + low.shape
    return pl.pallas_call(
        functools.partial(sum_kernel, cols),
        out_shape=(
            jax.ShapeDtypeStruct((share, count_tok), jnp.float32),
            jax.ShapeDtypeStruct(low.shape, jnp.float32),
        ),
        in_specs=[VMEM] * 2,
        out_specs=(VMEM, VMEM),
        scratch_shapes=[
            pltpu.VMEM(slots, jnp.bfloat16),
            pltpu.VMEM(slots, jnp.bfloat16),
            pltpu.VMEM(low_slots, jnp.float32),
            pltpu.VMEM(low_slots, jnp.float32),
        ]
        + [pltpu.SemaphoreType.DMA((2, hops))] * 4,
        compiler_params=pltpu.CompilerParams(collective_id=1, has_side_effects=True),
    )(parts, low)


def body(
    tokens,
    w_gate,
    w_up,
    w_down,
    adp_down,
    adp_up,
    expert_ids,
    gate_vals,
    lengths,
    perm,
    req_adapter,
):
    count_tok = tokens.shape[0]
    share = tokens.shape[1]
    rows_count = lax.axis_size("row")
    cols_count = lax.axis_size("col")
    experts = 2 * rows_count
    parts = cols_count // 2
    which = lax.axis_index("col") // parts
    topk = expert_ids.shape[1]
    capacity = max(2, (4 * count_tok * topk + 3 * experts - 1) // (3 * experts))
    slots = rows_count * capacity
    features = cols_count * share
    rank = adp_down.shape[1]
    own_adapters = adp_down.shape[0]
    adapters = own_adapters * rows_count

    tokens_t = tokens.T
    maps = jnp.concatenate(
        [adp_down.reshape(own_adapters * rank, share), adp_up.reshape(own_adapters * rank, share)]
    )
    full_t, maps = gather(tokens_t, maps)
    full_t = full_t.reshape(features, count_tok)

    flat_ids = expert_ids.reshape(-1)
    onehot = (flat_ids[:, None] == jnp.arange(experts, dtype=jnp.int32)[None, :]).astype(jnp.int32)
    slot = jnp.sum(onehot * jnp.cumsum(onehot, axis=0), axis=1) - 1
    place = jnp.where(flat_ids % 2 == which, (flat_ids // 2) * capacity + slot, slots)
    place = place.reshape(count_tok, topk).T
    targets = jnp.arange(slots, dtype=jnp.int32)
    hit = targets[:, None, None] == place[None, :, :]
    dispatch = jnp.any(hit, axis=1).astype(jnp.bfloat16)
    combine = jnp.sum(jnp.where(hit, gate_vals.T[None, :, :], jnp.float32(0.0)), axis=1)
    combine = jnp.concatenate(split_pair(combine), axis=1)

    outgoing = contract(dispatch, full_t, 1, 1).astype(jnp.bfloat16)
    outgoing = outgoing.reshape(rows_count, capacity, features)
    mine = lax.all_to_all(outgoing, "row", split_axis=0, concat_axis=0, tiled=True)
    mine = mine.reshape(slots, features)
    gate = contract(mine, w_gate[0], 1, 1)
    upper = contract(mine, w_up[0], 1, 1)
    hidden = (jax.nn.silu(gate) * upper).astype(jnp.bfloat16)
    partial_out = contract(hidden, w_down[0], 1, 0).astype(jnp.bfloat16)
    partial_out = partial_out.reshape(rows_count, capacity, features)
    returned = lax.all_to_all(partial_out, "row", split_axis=0, concat_axis=0, tiled=True)
    returned = returned.reshape(slots, features)
    routed_t = contract(returned, combine, 0, 0)
    routed_t = routed_t[:, :count_tok] + routed_t[:, count_tok:]

    maps = maps.reshape(rows_count, 2, own_adapters * rank, share)
    down_all = maps[:, 0].reshape(adapters * rank, share)
    up_all = maps[:, 1].reshape(adapters * rank, share)
    nreq = lengths.shape[0]
    ends = jnp.cumsum(lengths)
    request = jnp.sum((perm[:, None] >= ends[None, :]).astype(jnp.int32), axis=1)
    adapter = jnp.sum(
        jnp.where(
            request[:, None] == jnp.arange(nreq, dtype=jnp.int32)[None, :], req_adapter[None, :], 0
        ),
        axis=1,
    )
    chosen = jnp.arange(adapters, dtype=jnp.int32)[:, None, None] == adapter[None, None, :]
    projected = contract(down_all, tokens_t, 1, 0).reshape(adapters, rank, count_tok)
    partial_low = jnp.sum(jnp.where(chosen, projected, jnp.float32(0.0)), axis=0)

    total, low = sum_shares(routed_t.reshape(cols_count, share, count_tok), partial_low)
    low = low.astype(jnp.bfloat16)
    expanded = jnp.where(chosen, low[None], jnp.bfloat16(0.0)).reshape(adapters * rank, count_tok)
    delta_t = contract(up_all, expanded, 0, 0)
    return (total + adapter_scale_factor * delta_t).T.astype(jnp.bfloat16)


def solution(mesh):
    in_specs = (
        P("row", "col"),
        P(("row", "col"), None, None),
        P(("row", "col"), None, None),
        P(("row", "col"), None, None),
        P("row", None, "col"),
        P("row", None, "col"),
        P("row", None),
        P("row", None),
        P(),
        P("row"),
        P(),
    )
    out_specs = P("row", "col")
    return jax.shard_map(body, mesh=mesh, in_specs=in_specs, out_specs=out_specs, check_vma=False)
```

```python
import functools
import math

import jax
import jax.numpy as jnp
from jax import lax
from jax.experimental import pallas as pl
from jax.experimental.pallas import tpu as pltpu
from jax.sharding import PartitionSpec as P

MESH = pl.DeviceIdType.MESH
VMEM = pl.BlockSpec(memory_space=pltpu.VMEM)

adapter_scale_factor = 2.0


def contract(left, right, left_dim, right_dim):
    return lax.dot_general(
        left, right, (((left_dim,), (right_dim,)), ((), ())), preferred_element_type=jnp.float32
    )


def split_pair(value):
    high = lax.reduce_precision(value, 8, 7)
    return high.astype(jnp.bfloat16), (value - high).astype(jnp.bfloat16)


def remote(src, dst, send_sem, recv_sem, axis_name, peer):
    return pltpu.make_async_remote_copy(
        src_ref=src,
        dst_ref=dst,
        send_sem=send_sem,
        recv_sem=recv_sem,
        device_id={axis_name: peer},
        device_id_type=MESH,
    )


def mixed(turn, rows):
    return turn * (13 if math.gcd(13, rows) == 1 else 1) % rows


def gather_kernel(
    rows, cols, tok_ref, maps_ref, full_ref, all_ref, own_sem, ring_send, ring_recv, row_send, row_recv
):
    me_r, me_c = lax.axis_index("row"), lax.axis_index("col")
    sides = (lax.rem(me_c + 1, cols), lax.rem(me_c + cols - 1, cols))
    hops = (cols // 2, cols - 1 - cols // 2)

    barrier = pltpu.get_barrier_semaphore()
    for side in sides:
        pl.semaphore_signal(barrier, inc=1, device_id={"col": side}, device_id_type=MESH)

    def greet(away, carry):
        peer = lax.rem(me_r + away, rows)
        pl.semaphore_signal(barrier, inc=1, device_id={"row": peer}, device_id_type=MESH)
        return carry

    lax.fori_loop(1, rows, greet, 0)
    pl.semaphore_wait(barrier, rows + 1)

    def shard(way, step):
        return lax.rem(me_c + cols - step, cols) if way == 0 else lax.rem(me_c + step, cols)

    def sending(way, step):
        at = full_ref.at[shard(way, step)]
        src = tok_ref if step == 0 else at
        return remote(src, at, ring_send.at[way, step], ring_recv.at[way, step], "col", sides[way])

    def arriving(way, step):
        at = full_ref.at[shard(way, step + 1)]
        return remote(at, at, ring_send.at[way, step], ring_recv.at[way, step], "col", sides[way])

    def row_copy(away, owner):
        at = all_ref.at[owner]
        peer = lax.rem(me_r + away, rows)
        return remote(maps_ref, at, row_send.at[away], row_recv.at[away], "row", peer)

    for way in range(2):
        sending(way, 0).start()
    own = (
        pltpu.make_async_copy(tok_ref, full_ref.at[me_c], own_sem.at[0]),
        pltpu.make_async_copy(maps_ref, all_ref.at[me_r], own_sem.at[1]),
    )
    for copy in own:
        copy.start()
    batch = -(-(rows - 1) // max(hops))
    for step in range(max(hops)):
        for turn in range(1 + step * batch, min(rows, 1 + (step + 1) * batch)):
            row_copy(mixed(turn, rows), me_r).start()
        for way in range(2):
            if step < hops[way]:
                arriving(way, step).wait_recv()
                if step + 1 < hops[way]:
                    sending(way, step + 1).start()
    for copy in own:
        copy.wait()
    for way in range(2):
        for step in range(hops[way]):
            sending(way, step).wait_send()

    def row_end(away, carry):
        copy = row_copy(away, lax.rem(me_r + rows - away, rows))
        copy.wait_recv()
        copy.wait_send()
        return carry

    lax.fori_loop(1, rows, row_end, 0)


def gather(tokens_t, maps):
    rows, cols = lax.axis_size("row"), lax.axis_size("col")
    return pl.pallas_call(
        functools.partial(gather_kernel, rows, cols),
        out_shape=(
            jax.ShapeDtypeStruct((cols,) + tokens_t.shape, tokens_t.dtype),
            jax.ShapeDtypeStruct((rows,) + maps.shape, maps.dtype),
        ),
        in_specs=[VMEM] * 2,
        out_specs=(VMEM, VMEM),
        scratch_shapes=[
            pltpu.SemaphoreType.DMA((2,)),
            pltpu.SemaphoreType.DMA((2, cols)),
            pltpu.SemaphoreType.DMA((2, cols)),
            pltpu.SemaphoreType.DMA((rows,)),
            pltpu.SemaphoreType.DMA((rows,)),
        ],
        compiler_params=pltpu.CompilerParams(collective_id=0, has_side_effects=True),
    )(tokens_t, maps)


def expert_kernel(
    rows, groups, pick_ref, full_ref, gate_ref, up_ref, down_ref, back_ref,
    out_buf, in_buf, part_buf, out_send, out_recv, back_send, back_recv,
):
    me = lax.axis_index("row")
    members = rows // groups
    capacity, features = back_ref.shape[1:]
    height = members * capacity
    width = math.gcd(features, 512)

    barrier = pltpu.get_barrier_semaphore()

    def greet(away, carry):
        peer = lax.rem(me + away, rows)
        pl.semaphore_signal(barrier, inc=1, device_id={"row": peer}, device_id_type=MESH)
        return carry

    lax.fori_loop(1, rows, greet, 0)

    def outward(turn):
        peer = lax.rem(me + mixed(turn, rows), rows)
        return remote(
            out_buf.at[turn], in_buf.at[turn], out_send.at[turn], out_recv.at[turn], "row", peer
        )

    def homeward(turn):
        peer = lax.rem(me + rows - mixed(turn, rows), rows)
        return remote(
            part_buf.at[turn], back_ref.at[turn], back_send.at[turn], back_recv.at[turn], "row", peer
        )

    def turns(group):
        return [turn for turn in range(group * members, (group + 1) * members) if turn > 0]

    for group in range(groups):
        first = group * members
        picks = pick_ref[group * height : (group + 1) * height, :]

        def fill(tile, carry):
            at = pl.multiple_of(tile * width, width)
            block = contract(picks, full_ref[pl.ds(at, width), :], 1, 1).astype(jnp.bfloat16)
            out_buf[first : first + members, :, pl.ds(at, width)] = block.reshape(
                members, capacity, width
            )
            return carry

        lax.fori_loop(0, features // width, fill, 0)
        if group == 0:
            pl.semaphore_wait(barrier, rows - 1)
        for turn in turns(group):
            outward(turn).start()
    in_buf[0] = out_buf[0]

    for group in range(groups):
        first = group * members
        for turn in turns(group):
            outward(turn).wait_recv()
        mine = in_buf[first : first + members].reshape(height, features)
        gate = contract(mine, gate_ref[...], 1, 1)
        upper = contract(mine, up_ref[...], 1, 1)
        hidden = (jax.nn.silu(gate) * upper).astype(jnp.bfloat16)

        def fill_part(tile, carry):
            at = pl.multiple_of(tile * width, width)
            block = contract(hidden, down_ref[:, pl.ds(at, width)], 1, 0).astype(jnp.bfloat16)
            part_buf[first : first + members, :, pl.ds(at, width)] = block.reshape(
                members, capacity, width
            )
            return carry

        lax.fori_loop(0, features // width, fill_part, 0)
        for turn in turns(group):
            homeward(turn).start()
    back_ref[0] = part_buf[0]
    for turn in range(1, rows):
        homeward(turn).wait_recv()
    for turn in range(1, rows):
        outward(turn).wait_send()
        homeward(turn).wait_send()


def run_experts(pick, full_t, gate, up, down):
    rows = lax.axis_size("row")
    features = full_t.shape[0]
    blocks = (rows, pick.shape[0] // rows, features)
    groups = math.gcd(rows, 4)
    return pl.pallas_call(
        functools.partial(expert_kernel, rows, groups),
        out_shape=jax.ShapeDtypeStruct(blocks, jnp.bfloat16),
        in_specs=[VMEM] * 5,
        out_specs=VMEM,
        scratch_shapes=[pltpu.VMEM(blocks, jnp.bfloat16)] * 3
        + [pltpu.SemaphoreType.DMA((rows,))] * 4,
        compiler_params=pltpu.CompilerParams(collective_id=2, has_side_effects=True),
    )(pick, full_t, gate, up, down)


def sum_kernel(
    cols, part_ref, low_ref, total_ref, low_total_ref,
    out_part, in_part, out_low, in_low, send_sem, recv_sem, low_send_sem, low_recv_sem,
):
    me = lax.axis_index("col")
    sides = (lax.rem(me + 1, cols), lax.rem(me + cols - 1, cols))
    half = cols // 2
    hops = (half, cols - 1 - half)

    barrier = pltpu.get_barrier_semaphore()
    for side in sides:
        pl.semaphore_signal(barrier, inc=1, device_id={"col": side}, device_id_type=MESH)
    pl.semaphore_wait(barrier, 2)

    def copies(way, step):
        return (
            remote(
                out_part.at[way, step], in_part.at[way, step],
                send_sem.at[way, step], recv_sem.at[way, step], "col", sides[way],
            ),
            remote(
                out_low.at[way, step], in_low.at[way, step],
                low_send_sem.at[way, step], low_recv_sem.at[way, step], "col", sides[way],
            ),
        )

    for step in range(max(hops)):
        for way in range(2):
            if step >= hops[way]:
                continue
            if way == 0:
                chunk = lax.rem(me + hops[0] - step, cols)
            else:
                chunk = lax.rem(me + cols - hops[1] + step, cols)
            value, low = part_ref[chunk], low_ref[...]
            if step > 0:
                for copy in copies(way, step - 1):
                    copy.wait_recv()
                value = value + in_part[way, step - 1].astype(jnp.float32)
                low = low + in_low[way, step - 1]
            out_part[way, step] = value.astype(jnp.bfloat16)
            out_low[way, step] = low
            for copy in copies(way, step):
                copy.start()
    total, low = part_ref[me], low_ref[...]
    for way in range(2):
        last = hops[way] - 1
        for copy in copies(way, last):
            copy.wait_recv()
        total = total + in_part[way, last].astype(jnp.float32)
        low = low + in_low[way, last]
    total_ref[...] = total
    low_total_ref[...] = low
    for way in range(2):
        for step in range(hops[way]):
            for copy in copies(way, step):
                copy.wait_send()


def sum_shares(parts, low):
    cols, share, count_tok = parts.shape
    hops = cols // 2
    slots = (2, hops, share, count_tok)
    low_slots = (2, hops) + low.shape
    return pl.pallas_call(
        functools.partial(sum_kernel, cols),
        out_shape=(
            jax.ShapeDtypeStruct((share, count_tok), jnp.float32),
            jax.ShapeDtypeStruct(low.shape, jnp.float32),
        ),
        in_specs=[VMEM] * 2,
        out_specs=(VMEM, VMEM),
        scratch_shapes=[
            pltpu.VMEM(slots, jnp.bfloat16),
            pltpu.VMEM(slots, jnp.bfloat16),
            pltpu.VMEM(low_slots, jnp.float32),
            pltpu.VMEM(low_slots, jnp.float32),
        ]
        + [pltpu.SemaphoreType.DMA((2, hops))] * 4,
        compiler_params=pltpu.CompilerParams(collective_id=1, has_side_effects=True),
    )(parts, low)


def body(
    tokens,
    w_gate,
    w_up,
    w_down,
    adp_down,
    adp_up,
    expert_ids,
    gate_vals,
    lengths,
    perm,
    req_adapter,
):
    count_tok = tokens.shape[0]
    share = tokens.shape[1]
    rows_count = lax.axis_size("row")
    cols_count = lax.axis_size("col")
    experts = 2 * rows_count
    parts = cols_count // 2
    which = lax.axis_index("col") // parts
    topk = expert_ids.shape[1]
    capacity = max(2, (4 * count_tok * topk + 3 * experts - 1) // (3 * experts))
    slots = rows_count * capacity
    features = cols_count * share
    rank = adp_down.shape[1]
    own_adapters = adp_down.shape[0]
    adapters = own_adapters * rows_count

    tokens_t = tokens.T
    maps = jnp.concatenate(
        [adp_down.reshape(own_adapters * rank, share), adp_up.reshape(own_adapters * rank, share)]
    )
    full_t, maps = gather(tokens_t, maps)
    full_t = full_t.reshape(features, count_tok)

    flat_ids = expert_ids.reshape(-1)
    onehot = (flat_ids[:, None] == jnp.arange(experts, dtype=jnp.int32)[None, :]).astype(jnp.int32)
    slot = jnp.sum(onehot * jnp.cumsum(onehot, axis=0), axis=1) - 1
    place = jnp.where(flat_ids % 2 == which, (flat_ids // 2) * capacity + slot, slots)
    place = place.reshape(count_tok, topk).T
    turn = jnp.arange(slots, dtype=jnp.int32)
    peer = (lax.axis_index("row") + mixed(turn // capacity, rows_count)) % rows_count
    targets = peer * capacity + turn % capacity
    hit = targets[:, None, None] == place[None, :, :]
    dispatch = jnp.any(hit, axis=1).astype(jnp.bfloat16)
    combine = jnp.sum(jnp.where(hit, gate_vals.T[None, :, :], jnp.float32(0.0)), axis=1)
    combine = jnp.concatenate(split_pair(combine), axis=1)

    returned = run_experts(dispatch, full_t, w_gate[0], w_up[0], w_down[0])
    returned = returned.reshape(slots, features)
    routed_t = contract(returned, combine, 0, 0)
    routed_t = routed_t[:, :count_tok] + routed_t[:, count_tok:]

    maps = maps.reshape(rows_count, 2, own_adapters * rank, share)
    down_all = maps[:, 0].reshape(adapters * rank, share)
    up_all = maps[:, 1].reshape(adapters * rank, share)
    nreq = lengths.shape[0]
    ends = jnp.cumsum(lengths)
    request = jnp.sum((perm[:, None] >= ends[None, :]).astype(jnp.int32), axis=1)
    adapter = jnp.sum(
        jnp.where(
            request[:, None] == jnp.arange(nreq, dtype=jnp.int32)[None, :], req_adapter[None, :], 0
        ),
        axis=1,
    )
    chosen = jnp.arange(adapters, dtype=jnp.int32)[:, None, None] == adapter[None, None, :]
    projected = contract(down_all, tokens_t, 1, 0).reshape(adapters, rank, count_tok)
    partial_low = jnp.sum(jnp.where(chosen, projected, jnp.float32(0.0)), axis=0)

    total, low = sum_shares(routed_t.reshape(cols_count, share, count_tok), partial_low)
    low = low.astype(jnp.bfloat16)
    expanded = jnp.where(chosen, low[None], jnp.bfloat16(0.0)).reshape(adapters * rank, count_tok)
    delta_t = contract(up_all, expanded, 0, 0)
    return (total + adapter_scale_factor * delta_t).T.astype(jnp.bfloat16)


def solution(mesh):
    in_specs = (
        P("row", "col"),
        P(("row", "col"), None, None),
        P(("row", "col"), None, None),
        P(("row", "col"), None, None),
        P("row", None, "col"),
        P("row", None, "col"),
        P("row", None),
        P("row", None),
        P(),
        P("row"),
        P(),
    )
    out_specs = P("row", "col")
    return jax.shard_map(body, mesh=mesh, in_specs=in_specs, out_specs=out_specs, check_vma=False)
```

```python
import functools
import math

import jax
import jax.numpy as jnp
from jax import lax
from jax.experimental import pallas as pl
from jax.experimental.pallas import tpu as pltpu
from jax.sharding import PartitionSpec as P

MESH = pl.DeviceIdType.MESH
VMEM = pl.BlockSpec(memory_space=pltpu.VMEM)

adapter_scale_factor = 2.0


def contract(left, right, left_dim, right_dim):
    return lax.dot_general(
        left, right, (((left_dim,), (right_dim,)), ((), ())), preferred_element_type=jnp.float32
    )


def remote(src, dst, send_sem, recv_sem, axis_name, peer):
    return pltpu.make_async_remote_copy(
        src_ref=src,
        dst_ref=dst,
        send_sem=send_sem,
        recv_sem=recv_sem,
        device_id={axis_name: peer},
        device_id_type=MESH,
    )


def mixed(turn, rows):
    return turn * (13 if math.gcd(13, rows) == 1 else 1) % rows


def expert_kernel(
    rows, cols, groups,
    tok_ref, adp_down_ref, adp_up_ref, ids_ref, vals_ref, perm_ref, lengths_ref, req_ref,
    gate_hbm, up_hbm, down_hbm,
    back_ref, comb_ref, all_ref, low_ref, adapter_ref,
    full_ref, maps_ref, pick_ref, out_buf, in_buf, part_buf, gate_ref, up_ref, down_ref,
    own_sem, ring_send, ring_recv, row_send, row_recv, out_send, out_recv, back_send, back_recv,
):
    me_r, me_c = lax.axis_index("row"), lax.axis_index("col")
    sides = (lax.rem(me_c + 1, cols), lax.rem(me_c + cols - 1, cols))
    hops = (cols // 2, cols - 1 - cols // 2)
    members = rows // groups
    capacity, features = back_ref.shape[1:]
    share, count_tok = tok_ref.shape
    topk = ids_ref.shape[0]
    height = members * capacity
    joined = math.gcd(cols, 4)
    width = joined * share

    barrier = pltpu.get_barrier_semaphore()
    for side in sides:
        pl.semaphore_signal(barrier, inc=1, device_id={"col": side}, device_id_type=MESH)

    def greet(away, carry):
        peer = lax.rem(me_r + away, rows)
        pl.semaphore_signal(barrier, inc=1, device_id={"row": peer}, device_id_type=MESH)
        return carry

    lax.fori_loop(1, rows, greet, 0)

    weights = (
        pltpu.make_async_copy(gate_hbm, gate_ref, own_sem.at[2]),
        pltpu.make_async_copy(up_hbm, up_ref, own_sem.at[3]),
        pltpu.make_async_copy(down_hbm, down_ref, own_sem.at[4]),
    )
    for copy in weights:
        copy.start()
    kept = adp_down_ref.shape[0]
    maps_ref[:kept] = adp_down_ref[...]
    maps_ref[kept:] = adp_up_ref[...]

    def shard(way, step):
        return lax.rem(me_c + cols - step, cols) if way == 0 else lax.rem(me_c + step, cols)

    def sending(way, step):
        at = full_ref.at[shard(way, step)]
        src = tok_ref if step == 0 else at
        return remote(src, at, ring_send.at[way, step], ring_recv.at[way, step], "col", sides[way])

    def arriving(way, step):
        at = full_ref.at[shard(way, step + 1)]
        return remote(at, at, ring_send.at[way, step], ring_recv.at[way, step], "col", sides[way])

    def row_copy(away, owner):
        at = all_ref.at[owner]
        peer = lax.rem(me_r + away, rows)
        return remote(maps_ref, at, row_send.at[away], row_recv.at[away], "row", peer)

    def outward(turn):
        peer = lax.rem(me_r + mixed(turn, rows), rows)
        return remote(
            out_buf.at[turn], in_buf.at[turn], out_send.at[turn], out_recv.at[turn], "row", peer
        )

    def homeward(turn):
        peer = lax.rem(me_r + rows - mixed(turn, rows), rows)
        return remote(
            part_buf.at[turn], back_ref.at[turn], back_send.at[turn], back_recv.at[turn], "row", peer
        )

    def turns(group):
        return [turn for turn in range(group * members, (group + 1) * members) if turn > 0]

    pl.semaphore_wait(barrier, rows + 1)
    for way in range(2):
        sending(way, 0).start()
    own = (
        pltpu.make_async_copy(tok_ref, full_ref.at[me_c], own_sem.at[0]),
        pltpu.make_async_copy(maps_ref, all_ref.at[me_r], own_sem.at[1]),
    )
    for copy in own:
        copy.start()

    turn_at = lax.broadcasted_iota(jnp.int32, (rows, count_tok), 0)
    peer_at = lax.rem(me_r + mixed(turn_at, rows), rows)
    expert_at = 2 * peer_at + me_c // (cols // 2)
    named = jnp.zeros((rows, count_tok), jnp.float32)
    value = jnp.zeros((rows, count_tok), jnp.float32)
    for k in range(topk):
        same = ids_ref[k : k + 1, :] == expert_at
        named = named + jnp.where(same, 1.0, 0.0)
        value = value + jnp.where(same, vals_ref[k : k + 1, :], 0.0)
    earlier = lax.broadcasted_iota(jnp.int32, (count_tok, count_tok), 0)
    later = lax.broadcasted_iota(jnp.int32, (count_tok, count_tok), 1)
    before = jnp.where(earlier < later, 1.0, 0.0).astype(jnp.bfloat16)
    slot = contract(named.astype(jnp.bfloat16), before, 1, 0).astype(jnp.int32)
    slot = jnp.where(named > 0.0, slot, capacity)
    place = lax.broadcasted_iota(jnp.int32, (rows, capacity, count_tok), 1)
    hit = place == slot[:, None, :]
    pick_ref[...] = (
        jnp.where(hit, 1.0, 0.0).reshape(rows * capacity, count_tok).astype(jnp.bfloat16)
    )
    comb = jnp.where(hit, value[:, None, :], 0.0).reshape(rows * capacity, count_tok)
    high = comb.astype(jnp.bfloat16)
    comb_ref[:, :count_tok] = high
    comb_ref[:, count_tok:] = (comb - high.astype(jnp.float32)).astype(jnp.bfloat16)

    end = jnp.int32(0)
    request = jnp.zeros((1, count_tok), jnp.int32)
    for i in range(lengths_ref.shape[0]):
        end = end + lengths_ref[i]
        request = request + jnp.where(perm_ref[...] >= end, 1, 0)
    adapter = jnp.zeros((1, count_tok), jnp.int32)
    for i in range(lengths_ref.shape[0]):
        adapter = adapter + jnp.where(request == i, req_ref[i], 0)
    adapter_ref[...] = adapter

    batch = -(-(rows - 1) // max(hops))
    for step in range(max(hops)):
        for way in range(2):
            if step < hops[way]:
                arriving(way, step).wait_recv()
                if step + 1 < hops[way]:
                    sending(way, step + 1).start()
        for turn in range(1 + step * batch, min(rows, 1 + (step + 1) * batch)):
            row_copy(mixed(turn, rows), me_r).start()
    for copy in own:
        copy.wait()

    for group in range(groups):
        first = group * members
        picks = pick_ref[group * height : (group + 1) * height, :]

        def fill(tile, carry):
            at = pl.multiple_of(tile * width, width)
            piece = full_ref[pl.ds(tile * joined, joined)].reshape(width, count_tok)
            block = contract(picks, piece, 1, 1).astype(jnp.bfloat16)
            out_buf[first : first + members, :, pl.ds(at, width)] = block.reshape(
                members, capacity, width
            )
            return carry

        lax.fori_loop(0, features // width, fill, 0)
        for turn in turns(group):
            outward(turn).start()
    in_buf[0] = out_buf[0]

    def row_end(away, carry):
        row_copy(away, lax.rem(me_r + rows - away, rows)).wait_recv()
        return carry

    lax.fori_loop(1, rows, row_end, 0)
    rank = low_ref.shape[0]
    own_adapters = kept // rank
    low_ref[...] = jnp.zeros_like(low_ref)

    def project(owner, carry):
        piece = all_ref[owner][:kept]
        projected = contract(piece, tok_ref[...], 1, 0)
        for i in range(own_adapters):
            chosen = adapter == owner * own_adapters + i
            low_ref[...] += jnp.where(chosen, projected[i * rank : (i + 1) * rank], 0.0)
        return carry

    lax.fori_loop(0, rows, project, 0)

    for copy in weights:
        copy.wait()
    for group in range(groups):
        first = group * members
        for turn in turns(group):
            outward(turn).wait_recv()
        mine = in_buf[first : first + members].reshape(height, features)
        gate = contract(mine, gate_ref[...], 1, 1)
        upper = contract(mine, up_ref[...], 1, 1)
        hidden = (jax.nn.silu(gate) * upper).astype(jnp.bfloat16)

        def fill_part(tile, carry):
            at = pl.multiple_of(tile * width, width)
            block = contract(hidden, down_ref[:, pl.ds(at, width)], 1, 0).astype(jnp.bfloat16)
            part_buf[first : first + members, :, pl.ds(at, width)] = block.reshape(
                members, capacity, width
            )
            return carry

        lax.fori_loop(0, features // width, fill_part, 0)
        for turn in turns(group):
            homeward(turn).start()
    back_ref[0] = part_buf[0]
    for turn in range(1, rows):
        homeward(turn).wait_recv()
    for way in range(2):
        for step in range(hops[way]):
            sending(way, step).wait_send()

    def row_sent(away, carry):
        row_copy(away, me_r).wait_send()
        return carry

    lax.fori_loop(1, rows, row_sent, 0)
    for turn in range(1, rows):
        outward(turn).wait_send()
        homeward(turn).wait_send()


def run_experts(
    capacity, tokens_t, adp_down, adp_up, ids, vals, perm, lengths, req_adapter, gate, up, down
):
    rows, cols = lax.axis_size("row"), lax.axis_size("col")
    share, count_tok = tokens_t.shape
    features = gate.shape[1]
    blocks = (rows, capacity, features)
    slots = rows * capacity
    rank = adp_down.shape[1]
    adp_down, adp_up = adp_down.reshape(-1, share), adp_up.reshape(-1, share)
    maps = (2 * adp_down.shape[0], share)
    groups = math.gcd(rows, 4)
    smem = pl.BlockSpec(memory_space=pltpu.SMEM)
    hbm = pl.BlockSpec(memory_space=pl.ANY)
    return pl.pallas_call(
        functools.partial(expert_kernel, rows, cols, groups),
        out_shape=(
            jax.ShapeDtypeStruct(blocks, jnp.bfloat16),
            jax.ShapeDtypeStruct((slots, 2 * count_tok), jnp.bfloat16),
            jax.ShapeDtypeStruct((rows,) + maps, jnp.bfloat16),
            jax.ShapeDtypeStruct((rank, count_tok), jnp.float32),
            jax.ShapeDtypeStruct((1, count_tok), jnp.int32),
        ),
        in_specs=[VMEM] * 6 + [smem] * 2 + [hbm] * 3,
        out_specs=(VMEM,) * 5,
        scratch_shapes=[
            pltpu.VMEM((cols, share, count_tok), jnp.bfloat16),
            pltpu.VMEM(maps, jnp.bfloat16),
            pltpu.VMEM((slots, count_tok), jnp.bfloat16),
            pltpu.VMEM(blocks, jnp.bfloat16),
            pltpu.VMEM(blocks, jnp.bfloat16),
            pltpu.VMEM(blocks, jnp.bfloat16),
            pltpu.VMEM(gate.shape, jnp.bfloat16),
            pltpu.VMEM(up.shape, jnp.bfloat16),
            pltpu.VMEM(down.shape, jnp.bfloat16),
            pltpu.SemaphoreType.DMA((5,)),
            pltpu.SemaphoreType.DMA((2, cols)),
            pltpu.SemaphoreType.DMA((2, cols)),
        ]
        + [pltpu.SemaphoreType.DMA((rows,))] * 6,
        compiler_params=pltpu.CompilerParams(collective_id=0, has_side_effects=True),
    )(tokens_t, adp_down, adp_up, ids, vals, perm, lengths, req_adapter, gate, up, down)


def sum_kernel(
    cols, part_ref, low_ref, total_ref, low_total_ref,
    out_part, in_part, out_low, in_low, send_sem, recv_sem, low_send_sem, low_recv_sem,
):
    me = lax.axis_index("col")
    sides = (lax.rem(me + 1, cols), lax.rem(me + cols - 1, cols))
    half = cols // 2
    hops = (half, cols - 1 - half)

    barrier = pltpu.get_barrier_semaphore()
    for side in sides:
        pl.semaphore_signal(barrier, inc=1, device_id={"col": side}, device_id_type=MESH)
    pl.semaphore_wait(barrier, 2)

    def copies(way, step):
        return (
            remote(
                out_part.at[way, step], in_part.at[way, step],
                send_sem.at[way, step], recv_sem.at[way, step], "col", sides[way],
            ),
            remote(
                out_low.at[way, step], in_low.at[way, step],
                low_send_sem.at[way, step], low_recv_sem.at[way, step], "col", sides[way],
            ),
        )

    for step in range(max(hops)):
        for way in range(2):
            if step >= hops[way]:
                continue
            if way == 0:
                chunk = lax.rem(me + hops[0] - step, cols)
            else:
                chunk = lax.rem(me + cols - hops[1] + step, cols)
            value, low = part_ref[chunk], low_ref[...]
            if step > 0:
                for copy in copies(way, step - 1):
                    copy.wait_recv()
                value = value + in_part[way, step - 1].astype(jnp.float32)
                low = low + in_low[way, step - 1]
            out_part[way, step] = value.astype(jnp.bfloat16)
            out_low[way, step] = low
            for copy in copies(way, step):
                copy.start()
    total, low = part_ref[me], low_ref[...]
    for way in range(2):
        last = hops[way] - 1
        for copy in copies(way, last):
            copy.wait_recv()
        total = total + in_part[way, last].astype(jnp.float32)
        low = low + in_low[way, last]
    total_ref[...] = total
    low_total_ref[...] = low
    for way in range(2):
        for step in range(hops[way]):
            for copy in copies(way, step):
                copy.wait_send()


def sum_shares(parts, low):
    cols, share, count_tok = parts.shape
    hops = cols // 2
    slots = (2, hops, share, count_tok)
    low_slots = (2, hops) + low.shape
    return pl.pallas_call(
        functools.partial(sum_kernel, cols),
        out_shape=(
            jax.ShapeDtypeStruct((share, count_tok), jnp.float32),
            jax.ShapeDtypeStruct(low.shape, jnp.float32),
        ),
        in_specs=[VMEM] * 2,
        out_specs=(VMEM, VMEM),
        scratch_shapes=[
            pltpu.VMEM(slots, jnp.bfloat16),
            pltpu.VMEM(slots, jnp.bfloat16),
            pltpu.VMEM(low_slots, jnp.float32),
            pltpu.VMEM(low_slots, jnp.float32),
        ]
        + [pltpu.SemaphoreType.DMA((2, hops))] * 4,
        compiler_params=pltpu.CompilerParams(collective_id=1, has_side_effects=True),
    )(parts, low)


def body(
    tokens,
    w_gate,
    w_up,
    w_down,
    adp_down,
    adp_up,
    expert_ids,
    gate_vals,
    lengths,
    perm,
    req_adapter,
):
    count_tok = tokens.shape[0]
    share = tokens.shape[1]
    rows_count = lax.axis_size("row")
    cols_count = lax.axis_size("col")
    experts = 2 * rows_count
    topk = expert_ids.shape[1]
    capacity = max(2, (4 * count_tok * topk + 3 * experts - 1) // (3 * experts))
    slots = rows_count * capacity
    rank = adp_down.shape[1]
    own_adapters = adp_down.shape[0]
    adapters = own_adapters * rows_count

    returned, combine, maps, partial_low, adapter = run_experts(
        capacity, tokens.T, adp_down, adp_up, expert_ids.T, gate_vals.T, perm[None],
        lengths, req_adapter, w_gate[0], w_up[0], w_down[0],
    )
    routed_t = contract(returned.reshape(slots, -1), combine, 0, 0)
    routed_t = routed_t[:, :count_tok] + routed_t[:, count_tok:]
    up_all = maps[:, own_adapters * rank :].reshape(adapters * rank, share)
    chosen = jnp.arange(adapters, dtype=jnp.int32)[:, None, None] == adapter[None]

    total, low = sum_shares(routed_t.reshape(cols_count, share, count_tok), partial_low)
    low = low.astype(jnp.bfloat16)
    expanded = jnp.where(chosen, low[None], jnp.bfloat16(0.0)).reshape(adapters * rank, count_tok)
    delta_t = contract(up_all, expanded, 0, 0)
    return (total + adapter_scale_factor * delta_t).T.astype(jnp.bfloat16)


def solution(mesh):
    in_specs = (
        P("row", "col"),
        P(("row", "col"), None, None),
        P(("row", "col"), None, None),
        P(("row", "col"), None, None),
        P("row", None, "col"),
        P("row", None, "col"),
        P("row", None),
        P("row", None),
        P(),
        P("row"),
        P(),
    )
    out_specs = P("row", "col")
    return jax.shard_map(body, mesh=mesh, in_specs=in_specs, out_specs=out_specs, check_vma=False)
```

```python
import functools
import math

import jax
import jax.numpy as jnp
from jax import lax
from jax.experimental import pallas as pl
from jax.experimental.pallas import tpu as pltpu
from jax.sharding import PartitionSpec as P

MESH = pl.DeviceIdType.MESH
VMEM = pl.BlockSpec(memory_space=pltpu.VMEM)

adapter_scale_factor = 2.0


def contract(left, right, left_dim, right_dim):
    return lax.dot_general(
        left, right, (((left_dim,), (right_dim,)), ((), ())), preferred_element_type=jnp.float32
    )


def remote(src, dst, send_sem, recv_sem, axis_name, peer):
    return pltpu.make_async_remote_copy(
        src_ref=src,
        dst_ref=dst,
        send_sem=send_sem,
        recv_sem=recv_sem,
        device_id={axis_name: peer},
        device_id_type=MESH,
    )


def mixed(turn, rows):
    return lax.rem(turn * (13 if math.gcd(13, rows) == 1 else 1), rows)


def expert_kernel(
    rows, cols, groups,
    tok_ref, adp_down_ref, adp_up_ref, ids_ref, vals_ref, perm_ref, lengths_ref, req_ref,
    gate_hbm, up_hbm, down_hbm,
    total_ref, low_total_ref, all_ref, adapter_ref,
    full_ref, maps_ref, pick_ref, comb_ref, out_buf, in_buf, part_buf, back_buf,
    gate_ref, up_ref, down_ref, gate_t, up_t, down_t, gate_acc, up_acc, low_ref, share_part,
    sum_out, sum_in, low_out, low_in,
    own_sem, ring_send, ring_recv, row_send, row_recv, out_send, out_recv, back_send, back_recv,
    sum_send, sum_recv, low_send, low_recv,
):
    me_r, me_c = lax.axis_index("row"), lax.axis_index("col")
    sides = (lax.rem(me_c + 1, cols), lax.rem(me_c + cols - 1, cols))
    hops = (cols // 2, cols - 1 - cols // 2)
    capacity, features = back_buf.shape[1:]
    slots = rows * capacity
    hidden_units = gate_ref.shape[0]
    share, count_tok = tok_ref.shape
    topk = ids_ref.shape[0]
    width = features // groups
    offsets = [(-2 * g - 1, -2 * g - 2, 2 * g, 2 * g + 1) for g in range(groups)]
    where = {off % cols: 4 * g + i for g in range(groups) for i, off in enumerate(offsets[g])}

    barrier = pltpu.get_barrier_semaphore()
    for side in sides:
        pl.semaphore_signal(barrier, inc=1, device_id={"col": side}, device_id_type=MESH)

    def greet(away, carry):
        peer = lax.rem(me_r + away, rows)
        pl.semaphore_signal(barrier, inc=1, device_id={"row": peer}, device_id_type=MESH)
        return carry

    lax.fori_loop(1, rows, greet, 0)

    weights = (
        pltpu.make_async_copy(gate_hbm, gate_ref, own_sem.at[2]),
        pltpu.make_async_copy(up_hbm, up_ref, own_sem.at[3]),
        pltpu.make_async_copy(down_hbm, down_ref, own_sem.at[4]),
    )
    for copy in weights:
        copy.start()
    kept = adp_down_ref.shape[0]
    maps_ref[:kept] = adp_down_ref[...]
    maps_ref[kept:] = adp_up_ref[...]

    def share_at(off):
        return lax.rem(me_c + cols + off, cols)

    def shard(way, step):
        return share_at(-step) if way == 0 else share_at(step)

    def sending(way, step):
        at = full_ref.at[shard(way, step)]
        src = tok_ref if step == 0 else at
        return remote(src, at, ring_send.at[way, step], ring_recv.at[way, step], "col", sides[way])

    def arriving(way, step):
        at = full_ref.at[shard(way, step + 1)]
        return remote(at, at, ring_send.at[way, step], ring_recv.at[way, step], "col", sides[way])

    def row_copy(away, owner):
        at = all_ref.at[owner]
        peer = lax.rem(me_r + away, rows)
        return remote(maps_ref, at, row_send.at[away], row_recv.at[away], "row", peer)

    def lanes(group):
        return pl.ds(group * width, width)

    def outward(group, turn):
        peer = lax.rem(me_r + mixed(turn, rows), rows)
        return remote(
            out_buf.at[turn, :, lanes(group)], in_buf.at[turn, :, lanes(group)],
            out_send.at[group, turn], out_recv.at[group, turn], "row", peer,
        )

    def homeward(group, turn):
        peer = lax.rem(me_r + rows - mixed(turn, rows), rows)
        return remote(
            part_buf.at[turn, :, lanes(group)], back_buf.at[turn, :, lanes(group)],
            back_send.at[group, turn], back_recv.at[group, turn], "row", peer,
        )

    def each_turn(do):
        def step(turn, carry):
            do(turn)
            return carry

        lax.fori_loop(1, rows, step, 0)

    def joined(ref, group):
        return jnp.concatenate([ref[share_at(off)] for off in offsets[group]], axis=0)

    pl.semaphore_wait(barrier, rows + 1)
    for way in range(2):
        sending(way, 0).start()
    own = (
        pltpu.make_async_copy(tok_ref, full_ref.at[me_c], own_sem.at[0]),
        pltpu.make_async_copy(maps_ref, all_ref.at[me_r], own_sem.at[1]),
    )
    for copy in own:
        copy.start()

    turn_at = lax.broadcasted_iota(jnp.int32, (rows, count_tok), 0)
    peer_at = lax.rem(me_r + mixed(turn_at, rows), rows)
    expert_at = 2 * peer_at + me_c // (cols // 2)
    named = jnp.zeros((rows, count_tok), jnp.float32)
    value = jnp.zeros((rows, count_tok), jnp.float32)
    for k in range(topk):
        same = ids_ref[k : k + 1, :] == expert_at
        named = named + jnp.where(same, 1.0, 0.0)
        value = value + jnp.where(same, vals_ref[k : k + 1, :], 0.0)
    earlier = lax.broadcasted_iota(jnp.int32, (count_tok, count_tok), 0)
    later = lax.broadcasted_iota(jnp.int32, (count_tok, count_tok), 1)
    before = jnp.where(earlier < later, 1.0, 0.0).astype(jnp.bfloat16)
    slot = contract(named.astype(jnp.bfloat16), before, 1, 0).astype(jnp.int32)
    slot = jnp.where(named > 0.0, slot, capacity)
    place = lax.broadcasted_iota(jnp.int32, (rows, capacity, count_tok), 1)
    hit = place == slot[:, None, :]
    pick_ref[...] = (
        jnp.where(hit, 1.0, 0.0).reshape(rows * capacity, count_tok).astype(jnp.bfloat16)
    )
    comb = jnp.where(hit, value[:, None, :], 0.0).reshape(rows * capacity, count_tok)
    high = comb.astype(jnp.bfloat16)
    comb_ref[:, :count_tok] = high
    comb_ref[:, count_tok:] = (comb - high.astype(jnp.float32)).astype(jnp.bfloat16)

    end = jnp.int32(0)
    request = jnp.zeros((1, count_tok), jnp.int32)
    for i in range(lengths_ref.shape[0]):
        end = end + lengths_ref[i]
        request = request + jnp.where(perm_ref[...] >= end, 1, 0)
    adapter = jnp.zeros((1, count_tok), jnp.int32)
    for i in range(lengths_ref.shape[0]):
        adapter = adapter + jnp.where(request == i, req_ref[i], 0)
    adapter_ref[...] = adapter

    for copy in own:
        copy.wait()

    def ring_step(way, step):
        if step < hops[way]:
            arriving(way, step).wait_recv()
            if step + 1 < hops[way]:
                sending(way, step + 1).start()

    def accumulate(group):
        each_turn(lambda turn: outward(group, turn).wait_recv())
        mine = in_buf[:, :, group * width : (group + 1) * width].reshape(slots, width)
        for acc, weight in ((gate_acc, gate_t), (up_acc, up_t)):
            product = contract(mine, joined(weight, group), 1, 0)
            if group == 0:
                acc[...] = product
            else:
                acc[...] += product

    for group in range(groups):
        ring_step(0, 2 * group)
        if group > 0:
            ring_step(1, 2 * group - 1)
        ring_step(1, 2 * group)
        ring_step(0, 2 * group + 1)
        block = contract(pick_ref[...], joined(full_ref, group), 1, 1).astype(jnp.bfloat16)
        block = block.reshape(rows, capacity, width)
        out_buf[:, :, group * width : (group + 1) * width] = block
        in_buf[0, :, group * width : (group + 1) * width] = block[0]
        each_turn(lambda turn: outward(group, turn).start())
        if group == 0:
            for copy in weights:
                copy.wait()
            for plain, turned in ((gate_ref, gate_t), (up_ref, up_t), (down_ref, down_t)):
                for part in range(groups):
                    tile = plain[:, part * width : (part + 1) * width]
                    turned[4 * part : 4 * part + 4] = tile.T.reshape(4, share, hidden_units)
            each_turn(lambda turn: row_copy(mixed(turn, rows), me_r).start())
    for group in range(groups - 1):
        accumulate(group)

    def row_end(away, carry):
        row_copy(away, lax.rem(me_r + rows - away, rows)).wait_recv()
        return carry

    lax.fori_loop(1, rows, row_end, 0)
    rank = low_ref.shape[0]
    own_adapters = kept // rank
    low_ref[...] = jnp.zeros_like(low_ref)

    def project(owner, carry):
        piece = all_ref[owner][:kept]
        projected = contract(piece, tok_ref[...], 1, 0)
        for i in range(own_adapters):
            chosen = adapter == owner * own_adapters + i
            low_ref[...] += jnp.where(chosen, projected[i * rank : (i + 1) * rank], 0.0)
        return carry

    lax.fori_loop(0, rows, project, 0)

    accumulate(groups - 1)
    hidden = (jax.nn.silu(gate_acc[...]) * up_acc[...]).astype(jnp.bfloat16)
    for group in reversed(range(groups)):
        block = contract(hidden, joined(down_t, group), 1, 1).astype(jnp.bfloat16)
        block = block.reshape(rows, capacity, width)
        part_buf[:, :, group * width : (group + 1) * width] = block
        back_buf[0, :, group * width : (group + 1) * width] = block[0]
        each_turn(lambda turn: homeward(group, turn).start())

    sum_hops = (hops[1], hops[0])

    def sums(way, step):
        return (
            remote(
                sum_out.at[way, step], sum_in.at[way, step],
                sum_send.at[way, step], sum_recv.at[way, step], "col", sides[way],
            ),
            remote(
                low_out.at[way, step], low_in.at[way, step],
                low_send.at[way, step], low_recv.at[way, step], "col", sides[way],
            ),
        )

    def sum_step(way, step):
        off = sum_hops[0] - step if way == 0 else step - sum_hops[1]
        value, low = share_part[where[off % cols]], low_ref[...]
        if step > 0:
            for copy in sums(way, step - 1):
                copy.wait_recv()
            value = value + sum_in[way, step - 1].astype(jnp.float32)
            low = low + low_in[way, step - 1]
        sum_out[way, step] = value.astype(jnp.bfloat16)
        low_out[way, step] = low
        for copy in sums(way, step):
            copy.start()

    for step in range(sum_hops[1]):
        if step % 2 == 0:
            group = groups - 1 - step // 2
            each_turn(lambda turn: homeward(group, turn).wait_recv())
            back = back_buf[:, :, group * width : (group + 1) * width].reshape(slots, width)
            both = contract(back, comb_ref[...], 0, 0)
            both = both[:, :count_tok] + both[:, count_tok:]
            share_part[4 * group : 4 * group + 4] = both.reshape(4, share, count_tok)
        sum_step(1, step)
        if step > 0:
            sum_step(0, step - 1)
    total, low = share_part[where[0]], low_ref[...]
    for way in range(2):
        last = sum_hops[way] - 1
        for copy in sums(way, last):
            copy.wait_recv()
        total = total + sum_in[way, last].astype(jnp.float32)
        low = low + low_in[way, last]
    total_ref[...] = total
    low_total_ref[...] = low

    for way in range(2):
        for step in range(hops[way]):
            sending(way, step).wait_send()
        for step in range(sum_hops[way]):
            for copy in sums(way, step):
                copy.wait_send()
    each_turn(lambda turn: row_copy(turn, me_r).wait_send())
    for group in range(groups):
        each_turn(lambda turn: outward(group, turn).wait_send())
        each_turn(lambda turn: homeward(group, turn).wait_send())


def run_experts(
    capacity, tokens_t, adp_down, adp_up, ids, vals, perm, lengths, req_adapter, gate, up, down
):
    rows, cols = lax.axis_size("row"), lax.axis_size("col")
    share, count_tok = tokens_t.shape
    hidden_units, features = gate.shape
    blocks = (rows, capacity, features)
    slots = rows * capacity
    rank = adp_down.shape[1]
    adp_down, adp_up = adp_down.reshape(-1, share), adp_up.reshape(-1, share)
    maps = (2 * adp_down.shape[0], share)
    groups = cols // 4
    hops = cols // 2
    smem = pl.BlockSpec(memory_space=pltpu.SMEM)
    hbm = pl.BlockSpec(memory_space=pl.ANY)
    turned = pltpu.VMEM((cols, share, hidden_units), jnp.bfloat16)
    partial_low = pltpu.VMEM((2, hops, rank, count_tok), jnp.float32)
    return pl.pallas_call(
        functools.partial(expert_kernel, rows, cols, groups),
        out_shape=(
            jax.ShapeDtypeStruct((share, count_tok), jnp.float32),
            jax.ShapeDtypeStruct((rank, count_tok), jnp.float32),
            jax.ShapeDtypeStruct((rows,) + maps, jnp.bfloat16),
            jax.ShapeDtypeStruct((1, count_tok), jnp.int32),
        ),
        in_specs=[VMEM] * 6 + [smem] * 2 + [hbm] * 3,
        out_specs=(VMEM,) * 4,
        scratch_shapes=[
            pltpu.VMEM((cols, share, count_tok), jnp.bfloat16),
            pltpu.VMEM(maps, jnp.bfloat16),
            pltpu.VMEM((slots, count_tok), jnp.bfloat16),
            pltpu.VMEM((slots, 2 * count_tok), jnp.bfloat16),
        ]
        + [pltpu.VMEM(blocks, jnp.bfloat16)] * 4
        + [pltpu.VMEM(gate.shape, jnp.bfloat16)] * 3
        + [turned] * 3
        + [pltpu.VMEM((slots, hidden_units), jnp.float32)] * 2
        + [
            pltpu.VMEM((rank, count_tok), jnp.float32),
            pltpu.VMEM((cols, share, count_tok), jnp.float32),
            pltpu.VMEM((2, hops, share, count_tok), jnp.bfloat16),
            pltpu.VMEM((2, hops, share, count_tok), jnp.bfloat16),
            partial_low,
            partial_low,
            pltpu.SemaphoreType.DMA((5,)),
            pltpu.SemaphoreType.DMA((2, cols)),
            pltpu.SemaphoreType.DMA((2, cols)),
            pltpu.SemaphoreType.DMA((rows,)),
            pltpu.SemaphoreType.DMA((rows,)),
        ]
        + [pltpu.SemaphoreType.DMA((groups, rows))] * 4
        + [pltpu.SemaphoreType.DMA((2, hops))] * 4,
        compiler_params=pltpu.CompilerParams(collective_id=0, has_side_effects=True),
    )(tokens_t, adp_down, adp_up, ids, vals, perm, lengths, req_adapter, gate, up, down)


def body(
    tokens,
    w_gate,
    w_up,
    w_down,
    adp_down,
    adp_up,
    expert_ids,
    gate_vals,
    lengths,
    perm,
    req_adapter,
):
    count_tok = tokens.shape[0]
    share = tokens.shape[1]
    rows_count = lax.axis_size("row")
    experts = 2 * rows_count
    topk = expert_ids.shape[1]
    capacity = max(2, (4 * count_tok * topk + 3 * experts - 1) // (3 * experts))
    rank = adp_down.shape[1]
    own_adapters = adp_down.shape[0]
    adapters = own_adapters * rows_count

    total, low, maps, adapter = run_experts(
        capacity, tokens.T, adp_down, adp_up, expert_ids.T, gate_vals.T, perm[None],
        lengths, req_adapter, w_gate[0], w_up[0], w_down[0],
    )
    up_all = maps[:, own_adapters * rank :].reshape(adapters * rank, share)
    chosen = jnp.arange(adapters, dtype=jnp.int32)[:, None, None] == adapter[None]

    low = low.astype(jnp.bfloat16)
    expanded = jnp.where(chosen, low[None], jnp.bfloat16(0.0)).reshape(adapters * rank, count_tok)
    delta_t = contract(up_all, expanded, 0, 0)
    return (total + adapter_scale_factor * delta_t).T.astype(jnp.bfloat16)


def solution(mesh):
    in_specs = (
        P("row", "col"),
        P(("row", "col"), None, None),
        P(("row", "col"), None, None),
        P(("row", "col"), None, None),
        P("row", None, "col"),
        P("row", None, "col"),
        P("row", None),
        P("row", None),
        P(),
        P("row"),
        P(),
    )
    out_specs = P("row", "col")
    return jax.shard_map(body, mesh=mesh, in_specs=in_specs, out_specs=out_specs, check_vma=False)
```

```python
import functools
import math

import jax
import jax.numpy as jnp
from jax import lax
from jax.experimental import pallas as pl
from jax.experimental.pallas import tpu as pltpu
from jax.sharding import PartitionSpec as P

MESH = pl.DeviceIdType.MESH
VMEM = pl.BlockSpec(memory_space=pltpu.VMEM)

adapter_scale_factor = 2.0


def contract(left, right, left_dim, right_dim):
    return lax.dot_general(
        left, right, (((left_dim,), (right_dim,)), ((), ())), preferred_element_type=jnp.float32
    )


def remote(src, dst, send_sem, recv_sem, axis_name, peer):
    return pltpu.make_async_remote_copy(
        src_ref=src,
        dst_ref=dst,
        send_sem=send_sem,
        recv_sem=recv_sem,
        device_id={axis_name: peer},
        device_id_type=MESH,
    )


def mixed(turn, rows):
    return lax.rem(turn * (13 if math.gcd(13, rows) == 1 else 1), rows)


def expert_kernel(
    rows, cols, groups,
    tok_ref, adp_down_ref, adp_up_ref, ids_ref, vals_ref, perm_ref, lengths_ref, req_ref,
    gate_hbm, up_hbm, down_hbm,
    total_ref, low_total_ref, up_all_ref, adapter_ref,
    all_ref, full_ref, maps_ref, pick_ref, comb_ref, out_buf, in_buf, part_buf, back_buf,
    gate_ref, up_ref, down_ref, gate_t, up_t, down_t, gate_acc, up_acc, low_ref, share_part,
    sum_out, sum_in, low_out, low_in,
    own_sem, ring_send, ring_recv, row_send, row_recv, out_send, out_recv, back_send, back_recv,
    pass_send, pass_recv, sum_send, sum_recv, low_send, low_recv,
):
    me_r, me_c = lax.axis_index("row"), lax.axis_index("col")
    sides = (lax.rem(me_c + 1, cols), lax.rem(me_c + cols - 1, cols))
    hops = (cols // 2, cols - 1 - cols // 2)
    capacity, features = back_buf.shape[1:]
    slots = rows * capacity
    hidden_units = gate_ref.shape[0]
    share, count_tok = tok_ref.shape
    topk = ids_ref.shape[0]
    width = features // groups
    offsets = [(-2 * g - 1, -2 * g - 2, 2 * g, 2 * g + 1) for g in range(groups)]
    where = {off % cols: 4 * g + i for g in range(groups) for i, off in enumerate(offsets[g])}

    barrier = pltpu.get_barrier_semaphore()
    for side in sides:
        pl.semaphore_signal(barrier, inc=1, device_id={"col": side}, device_id_type=MESH)

    def greet(away, carry):
        peer = lax.rem(me_r + away, rows)
        pl.semaphore_signal(barrier, inc=1, device_id={"row": peer}, device_id_type=MESH)
        return carry

    lax.fori_loop(1, rows, greet, 0)

    weights = (
        pltpu.make_async_copy(gate_hbm, gate_ref, own_sem.at[2]),
        pltpu.make_async_copy(up_hbm, up_ref, own_sem.at[3]),
        pltpu.make_async_copy(down_hbm, down_ref, own_sem.at[4]),
    )
    for copy in weights:
        copy.start()
    kept = adp_down_ref.shape[0]
    maps_ref[:kept] = adp_down_ref[...]
    maps_ref[kept:] = adp_up_ref[...]

    def share_at(off):
        return lax.rem(me_c + cols + off, cols)

    def shard(way, step):
        return share_at(-step) if way == 0 else share_at(step)

    def sending(way, step):
        at = full_ref.at[shard(way, step)]
        src = tok_ref if step == 0 else at
        return remote(src, at, ring_send.at[way, step], ring_recv.at[way, step], "col", sides[way])

    def arriving(way, step):
        at = full_ref.at[shard(way, step + 1)]
        return remote(at, at, ring_send.at[way, step], ring_recv.at[way, step], "col", sides[way])

    pairs = rows // 2
    partner = me_r + 1 - 2 * lax.rem(me_r, 2)

    def owner_at(device, turn):
        return lax.rem(device + rows - 2 * turn, rows)

    def row_copy(turn, owner):
        at = all_ref.at[owner]
        peer = lax.rem(me_r + 2 * turn, rows)
        return remote(maps_ref, at, row_send.at[turn], row_recv.at[turn], "row", peer)

    def handing(turn):
        at = all_ref.at[owner_at(me_r, turn)]
        return remote(at, at, pass_send.at[turn], pass_recv.at[turn], "row", partner)

    def handed(turn):
        at = all_ref.at[owner_at(partner, turn)]
        return remote(at, at, pass_send.at[turn], pass_recv.at[turn], "row", partner)

    def each_pair(do):
        def step(turn, carry):
            do(turn)
            return carry

        lax.fori_loop(1, pairs, step, 0)

    def lanes(group):
        return pl.ds(group * width, width)

    def outward(group, turn):
        peer = lax.rem(me_r + mixed(turn, rows), rows)
        return remote(
            out_buf.at[turn, :, lanes(group)], in_buf.at[turn, :, lanes(group)],
            out_send.at[group, turn], out_recv.at[group, turn], "row", peer,
        )

    def homeward(group, turn):
        peer = lax.rem(me_r + rows - mixed(turn, rows), rows)
        return remote(
            part_buf.at[turn, :, lanes(group)], back_buf.at[turn, :, lanes(group)],
            back_send.at[group, turn], back_recv.at[group, turn], "row", peer,
        )

    def each_turn(do):
        def step(turn, carry):
            do(turn)
            return carry

        lax.fori_loop(1, rows, step, 0)

    def joined(ref, group):
        return jnp.concatenate([ref[share_at(off)] for off in offsets[group]], axis=0)

    pl.semaphore_wait(barrier, rows + 1)
    for way in range(2):
        sending(way, 0).start()
    own = (
        pltpu.make_async_copy(tok_ref, full_ref.at[me_c], own_sem.at[0]),
        pltpu.make_async_copy(maps_ref, all_ref.at[me_r], own_sem.at[1]),
    )
    for copy in own:
        copy.start()
    each_pair(lambda turn: row_copy(turn, me_r).start())

    turn_at = lax.broadcasted_iota(jnp.int32, (rows, count_tok), 0)
    peer_at = lax.rem(me_r + mixed(turn_at, rows), rows)
    expert_at = 2 * peer_at + me_c // (cols // 2)
    named = jnp.zeros((rows, count_tok), jnp.float32)
    value = jnp.zeros((rows, count_tok), jnp.float32)
    for k in range(topk):
        same = ids_ref[k : k + 1, :] == expert_at
        named = named + jnp.where(same, 1.0, 0.0)
        value = value + jnp.where(same, vals_ref[k : k + 1, :], 0.0)
    earlier = lax.broadcasted_iota(jnp.int32, (count_tok, count_tok), 0)
    later = lax.broadcasted_iota(jnp.int32, (count_tok, count_tok), 1)
    before = jnp.where(earlier < later, 1.0, 0.0).astype(jnp.bfloat16)
    slot = contract(named.astype(jnp.bfloat16), before, 1, 0).astype(jnp.int32)
    slot = jnp.where(named > 0.0, slot, capacity)
    place = lax.broadcasted_iota(jnp.int32, (rows, capacity, count_tok), 1)
    hit = place == slot[:, None, :]
    pick_ref[...] = (
        jnp.where(hit, 1.0, 0.0).reshape(rows * capacity, count_tok).astype(jnp.bfloat16)
    )
    comb = jnp.where(hit, value[:, None, :], 0.0).reshape(rows * capacity, count_tok)
    high = comb.astype(jnp.bfloat16)
    comb_ref[:, :count_tok] = high
    comb_ref[:, count_tok:] = (comb - high.astype(jnp.float32)).astype(jnp.bfloat16)

    end = jnp.int32(0)
    request = jnp.zeros((1, count_tok), jnp.int32)
    for i in range(lengths_ref.shape[0]):
        end = end + lengths_ref[i]
        request = request + jnp.where(perm_ref[...] >= end, 1, 0)
    adapter = jnp.zeros((1, count_tok), jnp.int32)
    for i in range(lengths_ref.shape[0]):
        adapter = adapter + jnp.where(request == i, req_ref[i], 0)
    adapter_ref[...] = adapter

    for copy in own:
        copy.wait()

    def ring_step(way, step):
        if step < hops[way]:
            arriving(way, step).wait_recv()
            if step + 1 < hops[way]:
                sending(way, step + 1).start()

    def accumulate(group):
        each_turn(lambda turn: outward(group, turn).wait_recv())
        mine = in_buf[:, :, group * width : (group + 1) * width].reshape(slots, width)
        for acc, weight in ((gate_acc, gate_t), (up_acc, up_t)):
            product = contract(mine, joined(weight, group), 1, 0)
            if group == 0:
                acc[...] = product
            else:
                acc[...] += product

    for group in range(groups):
        ring_step(0, 2 * group)
        if group > 0:
            ring_step(1, 2 * group - 1)
        ring_step(1, 2 * group)
        ring_step(0, 2 * group + 1)
        block = contract(pick_ref[...], joined(full_ref, group), 1, 1).astype(jnp.bfloat16)
        block = block.reshape(rows, capacity, width)
        out_buf[:, :, group * width : (group + 1) * width] = block
        in_buf[0, :, group * width : (group + 1) * width] = block[0]
        each_turn(lambda turn: outward(group, turn).start())
        if group == 0:
            for copy in weights:
                copy.wait()
            for plain, turned in ((gate_ref, gate_t), (up_ref, up_t), (down_ref, down_t)):
                for part in range(groups):
                    tile = plain[:, part * width : (part + 1) * width]
                    turned[4 * part : 4 * part + 4] = tile.T.reshape(4, share, hidden_units)
    handing(0).start()

    def hand_on(turn):
        row_copy(turn, owner_at(me_r, turn)).wait_recv()
        handing(turn).start()

    each_pair(hand_on)
    for group in range(groups - 1):
        accumulate(group)

    for turn in range(pairs):
        handed(turn).wait_recv()
    rank = low_ref.shape[0]
    own_adapters = kept // rank
    low_ref[...] = jnp.zeros_like(low_ref)

    def project(owner, carry):
        piece = all_ref[owner]
        up_all_ref[owner] = piece[kept:]
        projected = contract(piece[:kept], tok_ref[...], 1, 0)
        for i in range(own_adapters):
            chosen = adapter == owner * own_adapters + i
            low_ref[...] += jnp.where(chosen, projected[i * rank : (i + 1) * rank], 0.0)
        return carry

    lax.fori_loop(0, rows, project, 0)

    accumulate(groups - 1)
    hidden = (jax.nn.silu(gate_acc[...]) * up_acc[...]).astype(jnp.bfloat16)
    for group in reversed(range(groups)):
        block = contract(hidden, joined(down_t, group), 1, 1).astype(jnp.bfloat16)
        block = block.reshape(rows, capacity, width)
        part_buf[:, :, group * width : (group + 1) * width] = block
        back_buf[0, :, group * width : (group + 1) * width] = block[0]
        each_turn(lambda turn: homeward(group, turn).start())

    sum_hops = (hops[1], hops[0])

    def sums(way, step):
        return (
            remote(
                sum_out.at[way, step], sum_in.at[way, step],
                sum_send.at[way, step], sum_recv.at[way, step], "col", sides[way],
            ),
            remote(
                low_out.at[way, step], low_in.at[way, step],
                low_send.at[way, step], low_recv.at[way, step], "col", sides[way],
            ),
        )

    def sum_step(way, step):
        off = sum_hops[0] - step if way == 0 else step - sum_hops[1]
        value, low = share_part[where[off % cols]], low_ref[...]
        if step > 0:
            for copy in sums(way, step - 1):
                copy.wait_recv()
            value = value + sum_in[way, step - 1].astype(jnp.float32)
            low = low + low_in[way, step - 1]
        sum_out[way, step] = value.astype(jnp.bfloat16)
        low_out[way, step] = low
        for copy in sums(way, step):
            copy.start()

    for step in range(sum_hops[1]):
        if step % 2 == 0:
            group = groups - 1 - step // 2
            each_turn(lambda turn: homeward(group, turn).wait_recv())
            back = back_buf[:, :, group * width : (group + 1) * width].reshape(slots, width)
            both = contract(back, comb_ref[...], 0, 0)
            both = both[:, :count_tok] + both[:, count_tok:]
            share_part[4 * group : 4 * group + 4] = both.reshape(4, share, count_tok)
        sum_step(1, step)
        if step > 0:
            sum_step(0, step - 1)
    total, low = share_part[where[0]], low_ref[...]
    for way in range(2):
        last = sum_hops[way] - 1
        for copy in sums(way, last):
            copy.wait_recv()
        total = total + sum_in[way, last].astype(jnp.float32)
        low = low + low_in[way, last]
    total_ref[...] = total
    low_total_ref[...] = low

    for way in range(2):
        for step in range(hops[way]):
            sending(way, step).wait_send()
        for step in range(sum_hops[way]):
            for copy in sums(way, step):
                copy.wait_send()
    each_pair(lambda turn: row_copy(turn, me_r).wait_send())
    for turn in range(pairs):
        handing(turn).wait_send()
    for group in range(groups):
        each_turn(lambda turn: outward(group, turn).wait_send())
        each_turn(lambda turn: homeward(group, turn).wait_send())


def run_experts(
    capacity, tokens_t, adp_down, adp_up, ids, vals, perm, lengths, req_adapter, gate, up, down
):
    rows, cols = lax.axis_size("row"), lax.axis_size("col")
    share, count_tok = tokens_t.shape
    hidden_units, features = gate.shape
    blocks = (rows, capacity, features)
    slots = rows * capacity
    rank = adp_down.shape[1]
    adp_down, adp_up = adp_down.reshape(-1, share), adp_up.reshape(-1, share)
    maps = (2 * adp_down.shape[0], share)
    groups = cols // 4
    hops = cols // 2
    smem = pl.BlockSpec(memory_space=pltpu.SMEM)
    hbm = pl.BlockSpec(memory_space=pl.ANY)
    turned = pltpu.VMEM((cols, share, hidden_units), jnp.bfloat16)
    partial_low = pltpu.VMEM((2, hops, rank, count_tok), jnp.float32)
    return pl.pallas_call(
        functools.partial(expert_kernel, rows, cols, groups),
        out_shape=(
            jax.ShapeDtypeStruct((share, count_tok), jnp.float32),
            jax.ShapeDtypeStruct((rank, count_tok), jnp.float32),
            jax.ShapeDtypeStruct((rows,) + adp_up.shape, jnp.bfloat16),
            jax.ShapeDtypeStruct((1, count_tok), jnp.int32),
        ),
        in_specs=[VMEM] * 6 + [smem] * 2 + [hbm] * 3,
        out_specs=(VMEM,) * 4,
        scratch_shapes=[
            pltpu.VMEM((rows,) + maps, jnp.bfloat16),
            pltpu.VMEM((cols, share, count_tok), jnp.bfloat16),
            pltpu.VMEM(maps, jnp.bfloat16),
            pltpu.VMEM((slots, count_tok), jnp.bfloat16),
            pltpu.VMEM((slots, 2 * count_tok), jnp.bfloat16),
        ]
        + [pltpu.VMEM(blocks, jnp.bfloat16)] * 4
        + [pltpu.VMEM(gate.shape, jnp.bfloat16)] * 3
        + [turned] * 3
        + [pltpu.VMEM((slots, hidden_units), jnp.float32)] * 2
        + [
            pltpu.VMEM((rank, count_tok), jnp.float32),
            pltpu.VMEM((cols, share, count_tok), jnp.float32),
            pltpu.VMEM((2, hops, share, count_tok), jnp.bfloat16),
            pltpu.VMEM((2, hops, share, count_tok), jnp.bfloat16),
            partial_low,
            partial_low,
            pltpu.SemaphoreType.DMA((5,)),
            pltpu.SemaphoreType.DMA((2, cols)),
            pltpu.SemaphoreType.DMA((2, cols)),
            pltpu.SemaphoreType.DMA((rows // 2,)),
            pltpu.SemaphoreType.DMA((rows // 2,)),
        ]
        + [pltpu.SemaphoreType.DMA((groups, rows))] * 4
        + [pltpu.SemaphoreType.DMA((rows // 2,))] * 2
        + [pltpu.SemaphoreType.DMA((2, hops))] * 4,
        compiler_params=pltpu.CompilerParams(collective_id=0, has_side_effects=True),
    )(tokens_t, adp_down, adp_up, ids, vals, perm, lengths, req_adapter, gate, up, down)


def body(
    tokens,
    w_gate,
    w_up,
    w_down,
    adp_down,
    adp_up,
    expert_ids,
    gate_vals,
    lengths,
    perm,
    req_adapter,
):
    count_tok = tokens.shape[0]
    share = tokens.shape[1]
    rows_count = lax.axis_size("row")
    experts = 2 * rows_count
    topk = expert_ids.shape[1]
    capacity = max(2, (4 * count_tok * topk + 3 * experts - 1) // (3 * experts))
    rank = adp_down.shape[1]
    own_adapters = adp_down.shape[0]
    adapters = own_adapters * rows_count

    total, low, up_all, adapter = run_experts(
        capacity, tokens.T, adp_down, adp_up, expert_ids.T, gate_vals.T, perm[None],
        lengths, req_adapter, w_gate[0], w_up[0], w_down[0],
    )
    up_all = up_all.reshape(adapters * rank, share)
    chosen = jnp.arange(adapters, dtype=jnp.int32)[:, None, None] == adapter[None]

    low = low.astype(jnp.bfloat16)
    expanded = jnp.where(chosen, low[None], jnp.bfloat16(0.0)).reshape(adapters * rank, count_tok)
    delta_t = contract(up_all, expanded, 0, 0)
    return (total + adapter_scale_factor * delta_t).T.astype(jnp.bfloat16)


def solution(mesh):
    in_specs = (
        P("row", "col"),
        P(("row", "col"), None, None),
        P(("row", "col"), None, None),
        P(("row", "col"), None, None),
        P("row", None, "col"),
        P("row", None, "col"),
        P("row", None),
        P("row", None),
        P(),
        P("row"),
        P(),
    )
    out_specs = P("row", "col")
    return jax.shard_map(body, mesh=mesh, in_specs=in_specs, out_specs=out_specs, check_vma=False)
```

```python
import functools
import math

import jax
import jax.numpy as jnp
from jax import lax
from jax.experimental import pallas as pl
from jax.experimental.pallas import tpu as pltpu
from jax.sharding import PartitionSpec as P

MESH = pl.DeviceIdType.MESH
VMEM = pl.BlockSpec(memory_space=pltpu.VMEM)

adapter_scale_factor = 2.0


def contract(left, right, left_dim, right_dim):
    return lax.dot_general(
        left, right, (((left_dim,), (right_dim,)), ((), ())), preferred_element_type=jnp.float32
    )


def remote(src, dst, send_sem, recv_sem, axis_name, peer):
    return pltpu.make_async_remote_copy(
        src_ref=src,
        dst_ref=dst,
        send_sem=send_sem,
        recv_sem=recv_sem,
        device_id={axis_name: peer},
        device_id_type=MESH,
    )


def mixed(turn, rows):
    return lax.rem(turn * (13 if math.gcd(13, rows) == 1 else 1), rows)


def expert_kernel(
    rows, cols, groups,
    tok_ref, adp_down_ref, adp_up_ref, ids_ref, vals_ref, perm_ref, lengths_ref, req_ref,
    gate_hbm, up_hbm, down_hbm,
    total_ref, low_total_ref, up_all_ref, adapter_ref,
    all_ref, full_ref, maps_ref, pick_ref, comb_ref, out_buf, in_buf, part_buf, back_buf,
    gate_ref, up_ref, down_ref, gate_t, up_t, down_t, gate_acc, up_acc, low_ref, share_part,
    sum_out, sum_in, low_out, low_in,
    own_sem, ring_send, ring_recv, row_send, row_recv, out_send, out_recv, back_send, back_recv,
    pass_send, pass_recv, sum_send, sum_recv, low_send, low_recv,
):
    me_r, me_c = lax.axis_index("row"), lax.axis_index("col")
    sides = (lax.rem(me_c + 1, cols), lax.rem(me_c + cols - 1, cols))
    hops = (cols // 2, cols - 1 - cols // 2)
    capacity, features = back_buf.shape[1:]
    slots = rows * capacity
    hidden_units = gate_ref.shape[0]
    share, count_tok = tok_ref.shape
    topk = ids_ref.shape[0]
    width = features // groups
    offsets = [(-2 * g - 1, -2 * g - 2, 2 * g, 2 * g + 1) for g in range(groups)]
    where = {off % cols: 4 * g + i for g in range(groups) for i, off in enumerate(offsets[g])}

    barrier = pltpu.get_barrier_semaphore()
    for side in sides:
        pl.semaphore_signal(barrier, inc=1, device_id={"col": side}, device_id_type=MESH)

    def greet(away, carry):
        peer = lax.rem(me_r + away, rows)
        pl.semaphore_signal(barrier, inc=1, device_id={"row": peer}, device_id_type=MESH)
        return carry

    lax.fori_loop(1, rows, greet, 0)

    weights = (
        pltpu.make_async_copy(gate_hbm, gate_ref, own_sem.at[2]),
        pltpu.make_async_copy(up_hbm, up_ref, own_sem.at[3]),
        pltpu.make_async_copy(down_hbm, down_ref, own_sem.at[4]),
    )
    for copy in weights:
        copy.start()
    kept = adp_down_ref.shape[0]
    maps_ref[:kept] = adp_down_ref[...]
    maps_ref[kept:] = adp_up_ref[...]

    def share_at(off):
        return lax.rem(me_c + cols + off, cols)

    def shard(way, step):
        return share_at(-step) if way == 0 else share_at(step)

    def sending(way, step):
        at = full_ref.at[shard(way, step)]
        src = tok_ref if step == 0 else at
        return remote(src, at, ring_send.at[way, step], ring_recv.at[way, step], "col", sides[way])

    def arriving(way, step):
        at = full_ref.at[shard(way, step + 1)]
        return remote(at, at, ring_send.at[way, step], ring_recv.at[way, step], "col", sides[way])

    pairs = rows // 2
    partner = me_r + 1 - 2 * lax.rem(me_r, 2)

    def owner_at(device, turn):
        return lax.rem(device + rows - 2 * turn, rows)

    def row_copy(turn, owner):
        at = all_ref.at[owner]
        peer = lax.rem(me_r + 2 * turn, rows)
        return remote(maps_ref, at, row_send.at[turn], row_recv.at[turn], "row", peer)

    def handing(turn):
        at = all_ref.at[owner_at(me_r, turn)]
        return remote(at, at, pass_send.at[turn], pass_recv.at[turn], "row", partner)

    def handed(turn):
        at = all_ref.at[owner_at(partner, turn)]
        return remote(at, at, pass_send.at[turn], pass_recv.at[turn], "row", partner)

    def each_pair(do):
        def step(turn, carry):
            do(turn)
            return carry

        lax.fori_loop(1, pairs, step, 0)

    def lanes(group):
        return pl.ds(group * width, width)

    def outward(group, turn):
        peer = lax.rem(me_r + mixed(turn, rows), rows)
        return remote(
            out_buf.at[turn, :, lanes(group)], in_buf.at[turn, :, lanes(group)],
            out_send.at[group, turn], out_recv.at[group, turn], "row", peer,
        )

    def homeward(group, turn):
        peer = lax.rem(me_r + rows - mixed(turn, rows), rows)
        return remote(
            part_buf.at[turn, :, lanes(group)], back_buf.at[turn, :, lanes(group)],
            back_send.at[group, turn], back_recv.at[group, turn], "row", peer,
        )

    def each_turn(do):
        def step(turn, carry):
            do(turn)
            return carry

        lax.fori_loop(1, rows, step, 0)

    def joined(ref, group):
        return jnp.concatenate([ref[share_at(off)] for off in offsets[group]], axis=0)

    pl.semaphore_wait(barrier, rows + 1)
    for way in range(2):
        sending(way, 0).start()
    own = (
        pltpu.make_async_copy(tok_ref, full_ref.at[me_c], own_sem.at[0]),
        pltpu.make_async_copy(maps_ref, all_ref.at[me_r], own_sem.at[1]),
    )
    for copy in own:
        copy.start()
    each_pair(lambda turn: row_copy(turn, me_r).start())

    turn_at = lax.broadcasted_iota(jnp.int32, (rows, count_tok), 0)
    peer_at = lax.rem(me_r + mixed(turn_at, rows), rows)
    expert_at = 2 * peer_at + me_c // (cols // 2)
    named = jnp.zeros((rows, count_tok), jnp.float32)
    value = jnp.zeros((rows, count_tok), jnp.float32)
    for k in range(topk):
        same = ids_ref[k : k + 1, :] == expert_at
        named = named + jnp.where(same, 1.0, 0.0)
        value = value + jnp.where(same, vals_ref[k : k + 1, :], 0.0)
    earlier = lax.broadcasted_iota(jnp.int32, (count_tok, count_tok), 0)
    later = lax.broadcasted_iota(jnp.int32, (count_tok, count_tok), 1)
    before = jnp.where(earlier < later, 1.0, 0.0).astype(jnp.bfloat16)
    slot = contract(named.astype(jnp.bfloat16), before, 1, 0).astype(jnp.int32)
    slot = jnp.where(named > 0.0, slot, capacity)
    place = lax.broadcasted_iota(jnp.int32, (rows, capacity, count_tok), 1)
    hit = place == slot[:, None, :]
    pick_ref[...] = (
        jnp.where(hit, 1.0, 0.0).reshape(rows * capacity, count_tok).astype(jnp.bfloat16)
    )
    comb = jnp.where(hit, value[:, None, :], 0.0).reshape(rows * capacity, count_tok)
    high = comb.astype(jnp.bfloat16)
    comb_ref[:, :count_tok] = high
    comb_ref[:, count_tok:] = (comb - high.astype(jnp.float32)).astype(jnp.bfloat16)

    end = jnp.int32(0)
    request = jnp.zeros((1, count_tok), jnp.int32)
    for i in range(lengths_ref.shape[0]):
        end = end + lengths_ref[i]
        request = request + jnp.where(perm_ref[...] >= end, 1, 0)
    adapter = jnp.zeros((1, count_tok), jnp.int32)
    for i in range(lengths_ref.shape[0]):
        adapter = adapter + jnp.where(request == i, req_ref[i], 0)
    adapter_ref[...] = adapter

    for copy in own:
        copy.wait()

    def ring_step(way, step):
        if step < hops[way]:
            arriving(way, step).wait_recv()
            if step + 1 < hops[way]:
                sending(way, step + 1).start()

    def accumulate(group):
        each_turn(lambda turn: outward(group, turn).wait_recv())
        mine = in_buf[:, :, group * width : (group + 1) * width].reshape(slots, width)
        for acc, weight in ((gate_acc, gate_t), (up_acc, up_t)):
            product = contract(mine, joined(weight, group), 1, 0)
            if group == 0:
                acc[...] = product
            else:
                acc[...] += product

    for group in range(groups):
        ring_step(0, 2 * group)
        if group > 0:
            ring_step(1, 2 * group - 1)
        ring_step(1, 2 * group)
        ring_step(0, 2 * group + 1)
        block = contract(pick_ref[...], joined(full_ref, group), 1, 1).astype(jnp.bfloat16)
        block = block.reshape(rows, capacity, width)
        out_buf[:, :, group * width : (group + 1) * width] = block
        in_buf[0, :, group * width : (group + 1) * width] = block[0]
        each_turn(lambda turn: outward(group, turn).start())
    handing(0).start()

    def hand_on(turn):
        row_copy(turn, owner_at(me_r, turn)).wait_recv()
        handing(turn).start()

    each_pair(hand_on)
    for copy in weights:
        copy.wait()
    for plain, turned in ((gate_ref, gate_t), (up_ref, up_t), (down_ref, down_t)):
        for part in range(groups):
            tile = plain[:, part * width : (part + 1) * width]
            turned[4 * part : 4 * part + 4] = tile.T.reshape(4, share, hidden_units)
    for group in range(groups - 1):
        accumulate(group)

    for turn in range(pairs):
        handed(turn).wait_recv()
    rank = low_ref.shape[0]
    own_adapters = kept // rank
    low_ref[...] = jnp.zeros_like(low_ref)

    def project(owner, carry):
        piece = all_ref[owner]
        up_all_ref[owner] = piece[kept:]
        projected = contract(piece[:kept], tok_ref[...], 1, 0)
        for i in range(own_adapters):
            chosen = adapter == owner * own_adapters + i
            low_ref[...] += jnp.where(chosen, projected[i * rank : (i + 1) * rank], 0.0)
        return carry

    lax.fori_loop(0, rows, project, 0)

    accumulate(groups - 1)
    hidden = (jax.nn.silu(gate_acc[...]) * up_acc[...]).astype(jnp.bfloat16)
    for group in reversed(range(groups)):
        block = contract(hidden, joined(down_t, group), 1, 1).astype(jnp.bfloat16)
        block = block.reshape(rows, capacity, width)
        part_buf[:, :, group * width : (group + 1) * width] = block
        back_buf[0, :, group * width : (group + 1) * width] = block[0]
        each_turn(lambda turn: homeward(group, turn).start())

    sum_hops = (hops[1], hops[0])

    def sums(way, step):
        return (
            remote(
                sum_out.at[way, step], sum_in.at[way, step],
                sum_send.at[way, step], sum_recv.at[way, step], "col", sides[way],
            ),
            remote(
                low_out.at[way, step], low_in.at[way, step],
                low_send.at[way, step], low_recv.at[way, step], "col", sides[way],
            ),
        )

    def sum_step(way, step):
        off = sum_hops[0] - step if way == 0 else step - sum_hops[1]
        value, low = share_part[where[off % cols]], low_ref[...]
        if step > 0:
            for copy in sums(way, step - 1):
                copy.wait_recv()
            value = value + sum_in[way, step - 1].astype(jnp.float32)
            low = low + low_in[way, step - 1]
        sum_out[way, step] = value.astype(jnp.bfloat16)
        low_out[way, step] = low
        for copy in sums(way, step):
            copy.start()

    for step in range(sum_hops[1]):
        if step % 2 == 0:
            group = groups - 1 - step // 2
            each_turn(lambda turn: homeward(group, turn).wait_recv())
            back = back_buf[:, :, group * width : (group + 1) * width].reshape(slots, width)
            both = contract(back, comb_ref[...], 0, 0)
            both = both[:, :count_tok] + both[:, count_tok:]
            share_part[4 * group : 4 * group + 4] = both.reshape(4, share, count_tok)
        sum_step(1, step)
        if step > 0:
            sum_step(0, step - 1)
    total, low = share_part[where[0]], low_ref[...]
    for way in range(2):
        last = sum_hops[way] - 1
        for copy in sums(way, last):
            copy.wait_recv()
        total = total + sum_in[way, last].astype(jnp.float32)
        low = low + low_in[way, last]
    total_ref[...] = total
    low_total_ref[...] = low

    for way in range(2):
        for step in range(hops[way]):
            sending(way, step).wait_send()
        for step in range(sum_hops[way]):
            for copy in sums(way, step):
                copy.wait_send()
    each_pair(lambda turn: row_copy(turn, me_r).wait_send())
    for turn in range(pairs):
        handing(turn).wait_send()
    for group in range(groups):
        each_turn(lambda turn: outward(group, turn).wait_send())
        each_turn(lambda turn: homeward(group, turn).wait_send())


def run_experts(
    capacity, tokens_t, adp_down, adp_up, ids, vals, perm, lengths, req_adapter, gate, up, down
):
    rows, cols = lax.axis_size("row"), lax.axis_size("col")
    share, count_tok = tokens_t.shape
    hidden_units, features = gate.shape
    blocks = (rows, capacity, features)
    slots = rows * capacity
    rank = adp_down.shape[1]
    adp_down, adp_up = adp_down.reshape(-1, share), adp_up.reshape(-1, share)
    maps = (2 * adp_down.shape[0], share)
    groups = cols // 4
    hops = cols // 2
    smem = pl.BlockSpec(memory_space=pltpu.SMEM)
    hbm = pl.BlockSpec(memory_space=pl.ANY)
    turned = pltpu.VMEM((cols, share, hidden_units), jnp.bfloat16)
    partial_low = pltpu.VMEM((2, hops, rank, count_tok), jnp.float32)
    return pl.pallas_call(
        functools.partial(expert_kernel, rows, cols, groups),
        out_shape=(
            jax.ShapeDtypeStruct((share, count_tok), jnp.float32),
            jax.ShapeDtypeStruct((rank, count_tok), jnp.float32),
            jax.ShapeDtypeStruct((rows,) + adp_up.shape, jnp.bfloat16),
            jax.ShapeDtypeStruct((1, count_tok), jnp.int32),
        ),
        in_specs=[VMEM] * 6 + [smem] * 2 + [hbm] * 3,
        out_specs=(VMEM,) * 4,
        scratch_shapes=[
            pltpu.VMEM((rows,) + maps, jnp.bfloat16),
            pltpu.VMEM((cols, share, count_tok), jnp.bfloat16),
            pltpu.VMEM(maps, jnp.bfloat16),
            pltpu.VMEM((slots, count_tok), jnp.bfloat16),
            pltpu.VMEM((slots, 2 * count_tok), jnp.bfloat16),
        ]
        + [pltpu.VMEM(blocks, jnp.bfloat16)] * 4
        + [pltpu.VMEM(gate.shape, jnp.bfloat16)] * 3
        + [turned] * 3
        + [pltpu.VMEM((slots, hidden_units), jnp.float32)] * 2
        + [
            pltpu.VMEM((rank, count_tok), jnp.float32),
            pltpu.VMEM((cols, share, count_tok), jnp.float32),
            pltpu.VMEM((2, hops, share, count_tok), jnp.bfloat16),
            pltpu.VMEM((2, hops, share, count_tok), jnp.bfloat16),
            partial_low,
            partial_low,
            pltpu.SemaphoreType.DMA((5,)),
            pltpu.SemaphoreType.DMA((2, cols)),
            pltpu.SemaphoreType.DMA((2, cols)),
            pltpu.SemaphoreType.DMA((rows // 2,)),
            pltpu.SemaphoreType.DMA((rows // 2,)),
        ]
        + [pltpu.SemaphoreType.DMA((groups, rows))] * 4
        + [pltpu.SemaphoreType.DMA((rows // 2,))] * 2
        + [pltpu.SemaphoreType.DMA((2, hops))] * 4,
        compiler_params=pltpu.CompilerParams(collective_id=0, has_side_effects=True),
    )(tokens_t, adp_down, adp_up, ids, vals, perm, lengths, req_adapter, gate, up, down)


def body(
    tokens,
    w_gate,
    w_up,
    w_down,
    adp_down,
    adp_up,
    expert_ids,
    gate_vals,
    lengths,
    perm,
    req_adapter,
):
    count_tok = tokens.shape[0]
    share = tokens.shape[1]
    rows_count = lax.axis_size("row")
    experts = 2 * rows_count
    topk = expert_ids.shape[1]
    capacity = max(2, (4 * count_tok * topk + 3 * experts - 1) // (3 * experts))
    rank = adp_down.shape[1]
    own_adapters = adp_down.shape[0]
    adapters = own_adapters * rows_count

    total, low, up_all, adapter = run_experts(
        capacity, tokens.T, adp_down, adp_up, expert_ids.T, gate_vals.T, perm[None],
        lengths, req_adapter, w_gate[0], w_up[0], w_down[0],
    )
    up_all = up_all.reshape(adapters * rank, share)
    chosen = jnp.arange(adapters, dtype=jnp.int32)[:, None, None] == adapter[None]

    low = low.astype(jnp.bfloat16)
    expanded = jnp.where(chosen, low[None], jnp.bfloat16(0.0)).reshape(adapters * rank, count_tok)
    delta_t = contract(up_all, expanded, 0, 0)
    return (total + adapter_scale_factor * delta_t).T.astype(jnp.bfloat16)


def solution(mesh):
    in_specs = (
        P("row", "col"),
        P(("row", "col"), None, None),
        P(("row", "col"), None, None),
        P(("row", "col"), None, None),
        P("row", None, "col"),
        P("row", None, "col"),
        P("row", None),
        P("row", None),
        P(),
        P("row"),
        P(),
    )
    out_specs = P("row", "col")
    return jax.shard_map(body, mesh=mesh, in_specs=in_specs, out_specs=out_specs, check_vma=False)
```
